32 devices in a mesh: kv: 4 (over z), req: 8 (over y, x, core).
Axes of the slice: x: 2, y: 2, z: 4, core: 2. Of those that a mesh axis runs over, the one named last changes fastest.
Arguments:
- query: bfloat16 [768, 4096], P('req', 'kv'), may hold values from -7 to 7
- latest_key_value: bfloat16 [2, 768, 512], P(None, 'req', 'kv'), may hold values from -5 to 5
- cache: bfloat16 [2, 393216, 512], P(None, 'req', 'kv'), may hold values from -6 to 6
- out_weight: bfloat16 [4096, 4096], P('kv'), may hold values from -0.5 to 0.5
- home: int32 [768], replicated, may hold values from 0 to 767, as said below
- pieces: int32 [2, 768], replicated, may hold values from 0 to 767, as said below
- lengths: int32 [768], replicated, may hold values from 1 to 1920, as said below
Outputs:
- projected: bfloat16 [768, 4096], P('req', 'kv')
The draws below stay inside these ranges and needn't reach their ends.
Inputs may be any that keep to these rules, and one draw needn't show every extreme that they name: A permutation of the home slots; slot g lies on owner g // 96. The requests i * 96 to (i + 1) * 96 - 1 have their homes on exactly 4 owners, exactly 24 on each. `pieces`: guest slot j lies on owner j // 96. The requests of each index of req have exactly 24 guest slots on each of 4 owners; a request has 4 guest slots or none. Every guest slot has 1 to 384 positions. `lengths`: every home slot gets 1 or more positions, and on every owner the slots take exactly 384 pages.
All inputs are finite; a program needn't handle non-finite values.
Results may differ from the reference program's by a relative error of at most 0.0055.
Values may be sent and summed in bfloat16 or wider, within the bound.
A program may use at most 192 MiB of HBM per device.

```python
import jax
import jax.numpy as jnp
from jax import lax

D = 4096
QUERY_HEADS = 32
KEY_VALUE_HEADS = 4
HEAD_WIDTH = 128
REQ_DEV = 96
SPLIT = 4
PAGE_POSITIONS = 128
EXTRA_DEV = 96
OWNER_PAGES = 384
REQUEST_TOTAL = 768
PIECES = 768
HOME_CAP = 24
PIECE_CAP = 24
TOKEN_TOTAL = 393216
N_REQ = 8


def owner_perms(key, length):

    def shuffle_one(subkey):
        return jax.random.permutation(subkey, length)
    return jax.vmap(shuffle_one)(jax.random.split(key, N_REQ)).astype(jnp.int32)


def pair_pages(count):
    list_index = jnp.arange(count, dtype=jnp.int32)
    pair_index = list_index // 2 % 3
    return jnp.where(list_index % 2 == 0, 1 + pair_index, 3 - pair_index).astype(jnp.int32)


def integer_tables(key):
    base_key = jax.random.fold_in(key, 7001)
    subkeys = jax.random.split(base_key, 11)
    device_ids = jnp.arange(N_REQ, dtype=jnp.int32)
    half_count = N_REQ // 2
    home_shift = jax.random.permutation(subkeys[0], N_REQ).astype(jnp.int32)[:half_count]
    piece_shift = jax.random.permutation(subkeys[1], N_REQ).astype(jnp.int32)[:half_count]
    send_order = owner_perms(subkeys[2], REQ_DEV)
    land_order = owner_perms(subkeys[3], REQ_DEV)
    home_group = send_order // HOME_CAP
    home_dest = (device_ids[:, None] + home_shift[home_group]) % N_REQ
    home_slot = land_order[home_dest, send_order]
    home = (home_dest * REQ_DEV + home_slot).reshape(REQUEST_TOTAL).astype(jnp.int32)
    long_count = EXTRA_DEV // SPLIT
    long_order = owner_perms(subkeys[4], REQ_DEV - 1)
    long_pick = jnp.concatenate([jnp.full((N_REQ, 1), REQ_DEV - 1, jnp.int32), long_order[:, :long_count - 1]], axis=1)
    piece_order = owner_perms(subkeys[5], EXTRA_DEV)
    guest_order = owner_perms(subkeys[6], EXTRA_DEV)
    position = jnp.broadcast_to(jnp.arange(EXTRA_DEV, dtype=jnp.int32)[None, :], (N_REQ, EXTRA_DEV))
    piece_group = position // PIECE_CAP
    piece_owner = (device_ids[:, None] + piece_shift[piece_group]) % N_REQ
    long_local = jnp.take_along_axis(long_pick, piece_order % long_count, axis=1)
    piece_request = device_ids[:, None] * REQ_DEV + long_local
    guest_slot = piece_owner * EXTRA_DEV + guest_order[piece_owner, position]
    request_of_slot = jnp.zeros((PIECES,), jnp.int32).at[guest_slot.reshape(-1)].set(piece_request.reshape(-1))
    list_index = jnp.arange(REQ_DEV, dtype=jnp.int32)
    page_list = pair_pages(REQ_DEV)
    count_perm = owner_perms(subkeys[7], REQ_DEV)
    target = home[REQUEST_TOTAL - 1]
    target_owner = target // REQ_DEV
    target_slot = target % REQ_DEV
    target_row = count_perm[target_owner]
    full_at = jnp.argmax((target_row == 1).astype(jnp.int32)).astype(jnp.int32)
    held = target_row[target_slot]
    new_row = jnp.where(list_index == target_slot, 1, jnp.where(list_index == full_at, held, target_row))
    count_perm = count_perm.at[target_owner].set(new_row.astype(jnp.int32))
    home_pages = page_list[count_perm]
    home_tail = jax.random.randint(subkeys[8], (N_REQ, REQ_DEV), 1, PAGE_POSITIONS + 1)
    home_tail = jnp.where(count_perm == 1, PAGE_POSITIONS, home_tail)
    home_slot_len = ((home_pages - 1) * PAGE_POSITIONS + home_tail).astype(jnp.int32)
    guest_list = pair_pages(EXTRA_DEV)
    guest_desc = (-jnp.sort(-guest_list)).astype(jnp.int32)
    is_target = request_of_slot.reshape(N_REQ, EXTRA_DEV) == REQUEST_TOTAL - 1
    guest_perm = owner_perms(subkeys[10], EXTRA_DEV)
    guest_score = jnp.where(is_target, position, EXTRA_DEV + guest_perm).astype(jnp.int32)
    guest_sorted = jnp.argsort(guest_score, axis=1).astype(jnp.int32)
    guest_rank = jnp.argsort(guest_sorted, axis=1).astype(jnp.int32)
    guest_pages = guest_desc[guest_rank]
    guest_tail = jax.random.randint(subkeys[9], (N_REQ, EXTRA_DEV), 1, PAGE_POSITIONS + 1)
    guest_tail = jnp.where(is_target, PAGE_POSITIONS, guest_tail)
    guest_slot_len = ((guest_pages - 1) * PAGE_POSITIONS + guest_tail).astype(jnp.int32)
    home_len = home_slot_len.reshape(REQUEST_TOTAL)
    guest_len = guest_slot_len.reshape(PIECES)
    guest_total = jnp.zeros((REQUEST_TOTAL,), jnp.int32).at[request_of_slot].add(guest_len)
    lengths = (home_len[home] + guest_total).astype(jnp.int32)
    pieces = jnp.stack([request_of_slot, guest_len]).astype(jnp.int32)
    return (home, pieces, lengths)


def draw_home(key, part):
    return integer_tables(key)[0]


def draw_pieces(key, part):
    return integer_tables(key)[1]


def draw_lengths(key, part):
    return integer_tables(key)[2]


def latest_pair(key):
    pair_random_key = jax.random.fold_in(key, 8201)
    return jax.random.truncated_normal(pair_random_key, -5.0, 5.0, (2, REQUEST_TOTAL, KEY_VALUE_HEADS * HEAD_WIDTH), jnp.float32)


def draw_latest_key_value(key, part):
    return latest_pair(key).astype(jnp.bfloat16)


def draw_query(key, part):
    group_width = QUERY_HEADS // KEY_VALUE_HEADS
    self_key = latest_pair(key)[0].reshape(REQUEST_TOTAL, KEY_VALUE_HEADS, 1, HEAD_WIDTH)
    random_key = jax.random.fold_in(key, 8301)
    random_part = jax.random.truncated_normal(random_key, -5.0, 5.0, (REQUEST_TOTAL, KEY_VALUE_HEADS, group_width, HEAD_WIDTH), jnp.float32)
    query_mix = random_part + 0.35 * self_key
    return query_mix.reshape(REQUEST_TOTAL, QUERY_HEADS * HEAD_WIDTH).astype(jnp.bfloat16)


def draw_cache(key, part):
    tensor_shape = (2, TOKEN_TOTAL, KEY_VALUE_HEADS, HEAD_WIDTH)
    random_key = jax.random.fold_in(key, 8501)
    filled_rows = jax.random.truncated_normal(random_key, -5.0, 5.0, tensor_shape, jnp.float32)
    return filled_rows.reshape(2, TOKEN_TOTAL, KEY_VALUE_HEADS * HEAD_WIDTH).astype(jnp.bfloat16)


def steps_of(own_key, dims, cuts, low, top_value):
    def one(dim, parts):
        steps = jax.random.uniform(jax.random.fold_in(jax.random.fold_in(own_key, 6), dim), (parts,), jnp.float32, low / len(cuts), top_value / len(cuts))
        return jnp.repeat(jnp.exp(steps), dims[dim] // parts).reshape((-1,) + (1,) * (len(dims) - dim - 1))

    factor_of = one(*cuts[0])
    for cut in cuts[1:]:
        factor_of = factor_of * one(*cut)
    return factor_of


def gaussian(key, dims, spread, reach, cuts=(), kind=jnp.bfloat16):
    loudness = steps_of(key, dims, cuts, -0.22, 0.18) if cuts else 1.0
    array = jax.random.normal(key, dims, jnp.float32) * spread * loudness
    return jnp.minimum(jnp.maximum(array, -reach), reach).astype(kind)


def setup_inputs(seed: int = 0) -> dict:
    key_list = jax.random.split(jax.random.key(seed), 8)
    query = draw_query(jax.random.fold_in(key_list[7], 71), 0)
    latest_key_value = draw_latest_key_value(jax.random.fold_in(key_list[7], 71), 0)
    cache = draw_cache(jax.random.fold_in(key_list[7], 71), 0)
    out_weight = gaussian(key_list[3], (QUERY_HEADS * HEAD_WIDTH, D), HEAD_WIDTH ** -0.5, 0.5, ((0, 4),))
    home = draw_home(jax.random.fold_in(key_list[7], 71), 0)
    pieces = draw_pieces(jax.random.fold_in(key_list[7], 71), 0)
    lengths = draw_lengths(jax.random.fold_in(key_list[7], 71), 0)
    return dict(query=query, latest_key_value=latest_key_value, cache=cache, out_weight=out_weight, home=home, pieces=pieces, lengths=lengths)


def slot_pages(slot_len, page_count):
    slot_count = slot_len.shape[0]
    per_slot = ((slot_len + PAGE_POSITIONS - 1) // PAGE_POSITIONS).astype(jnp.int32)
    slot_end = jnp.cumsum(per_slot).astype(jnp.int32)
    slot_begin = (slot_end - per_slot).astype(jnp.int32)
    page_index = jnp.arange(page_count, dtype=jnp.int32)
    page_slot = jnp.sum((slot_end[None, :] <= page_index[:, None]).astype(jnp.int32), axis=1).astype(jnp.int32)
    slot_hot = jnp.arange(slot_count, dtype=jnp.int32)[:, None] == page_slot[None, :]
    page_begin = jnp.sum(jnp.where(slot_hot, slot_begin[:, None], 0), axis=0).astype(jnp.int32)
    page_length = jnp.sum(jnp.where(slot_hot, slot_len[:, None], 0), axis=0).astype(jnp.int32)
    page_used = jnp.clip(page_length - (page_index - page_begin) * PAGE_POSITIONS, 0, PAGE_POSITIONS).astype(jnp.int32)
    return page_slot, slot_hot, page_used


def reference(query, latest_key_value, cache, out_weight, home, pieces, lengths):
    group_width = QUERY_HEADS // KEY_VALUE_HEADS
    slot_count = REQ_DEV + EXTRA_DEV
    scale_multiplier = HEAD_WIDTH ** -0.5
    batch_index = jnp.arange(REQUEST_TOTAL, dtype=jnp.int32)
    inverse = jnp.zeros((REQUEST_TOTAL,), jnp.int32).at[home].set(batch_index)
    piece_req = pieces[0]
    piece_len = pieces[1]
    guest_total = jnp.zeros((REQUEST_TOTAL,), jnp.int32).at[piece_req].add(piece_len)
    query_complete = query.astype(jnp.float32).reshape(REQUEST_TOTAL, KEY_VALUE_HEADS, group_width, HEAD_WIDTH)
    cached_rows = cache.reshape(2, N_REQ, OWNER_PAGES, PAGE_POSITIONS, KEY_VALUE_HEADS, HEAD_WIDTH)

    def one_owner(owner_index):
        home_rows = lax.dynamic_slice_in_dim(inverse, owner_index * REQ_DEV, REQ_DEV)
        guest_rows = lax.dynamic_slice_in_dim(piece_req, owner_index * EXTRA_DEV, EXTRA_DEV)
        guest_len = lax.dynamic_slice_in_dim(piece_len, owner_index * EXTRA_DEV, EXTRA_DEV)
        slot_rows = jnp.concatenate([home_rows, guest_rows]).astype(jnp.int32)
        home_len = lengths[home_rows] - guest_total[home_rows]
        slot_len = jnp.concatenate([home_len, guest_len]).astype(jnp.int32)
        page_slot, slot_hot, page_used = slot_pages(slot_len, OWNER_PAGES)
        page_query = query_complete[slot_rows[page_slot]]
        page_keys = cached_rows[0, owner_index].astype(jnp.float32)
        page_values = cached_rows[1, owner_index].astype(jnp.float32)
        scores = jnp.einsum("pkgd,ptkd->pkgt", page_query, page_keys) * scale_multiplier
        in_use = (jnp.arange(PAGE_POSITIONS, dtype=jnp.int32)[None, :] < page_used[:, None])[:, None, None, :]
        scores = jnp.where(in_use, scores, -jnp.inf)
        slot_maximum = jax.ops.segment_max(jnp.max(scores, axis=-1), page_slot, num_segments=slot_count)
        weights = jnp.where(in_use, jnp.exp(scores - slot_maximum[page_slot][..., None]), 0.0).astype(jnp.bfloat16)
        weights = lax.optimization_barrier(weights).astype(jnp.float32)
        slot_total_sum = jax.ops.segment_sum(jnp.sum(weights, axis=-1), page_slot, num_segments=slot_count)
        page_out = jnp.einsum("pkgt,ptkd->pkgd", weights, page_values)
        slot_out = jax.ops.segment_sum(page_out, page_slot, num_segments=slot_count)
        slot_average = (slot_out / slot_total_sum[..., None]).astype(jnp.bfloat16)
        slot_average = lax.optimization_barrier(slot_average).astype(jnp.float32)
        return slot_rows, slot_maximum, slot_total_sum, slot_average

    slot_rows, slot_maximum, slot_total_sum, slot_average = lax.map(one_owner, jnp.arange(N_REQ, dtype=jnp.int32))
    slot_rows = slot_rows.reshape(-1)
    slot_maximum = slot_maximum.reshape(-1, KEY_VALUE_HEADS, group_width)
    slot_total_sum = slot_total_sum.reshape(-1, KEY_VALUE_HEADS, group_width)
    slot_average = slot_average.reshape(-1, KEY_VALUE_HEADS, group_width, HEAD_WIDTH)
    latest_keys = latest_key_value[0].astype(jnp.float32).reshape(REQUEST_TOTAL, KEY_VALUE_HEADS, HEAD_WIDTH)
    latest_values = latest_key_value[1].astype(jnp.float32).reshape(REQUEST_TOTAL, KEY_VALUE_HEADS, HEAD_WIDTH)
    self_score = jnp.einsum("iqcu,iqu->iqc", query_complete, latest_keys) * scale_multiplier
    row_top = jnp.maximum(jax.ops.segment_max(slot_maximum, slot_rows, num_segments=REQUEST_TOTAL), self_score)
    factor = jnp.exp(slot_maximum - row_top[slot_rows])
    own_factor = jnp.exp(self_score - row_top)
    slot_coef = slot_total_sum * factor
    denominator = jax.ops.segment_sum(slot_coef, slot_rows, num_segments=REQUEST_TOTAL) + own_factor
    numerator = jax.ops.segment_sum(slot_average * slot_coef[..., None], slot_rows, num_segments=REQUEST_TOTAL)
    numerator = numerator + latest_values[:, :, None, :] * own_factor[..., None]
    attended = (numerator / denominator[..., None]).astype(jnp.bfloat16).reshape(REQUEST_TOTAL, QUERY_HEADS * HEAD_WIDTH)
    return jnp.dot(attended, out_weight, preferred_element_type=jnp.float32).astype(jnp.bfloat16)
```

```python
import functools

import jax
import jax.numpy as jnp
from jax import lax
from jax.experimental import pallas as pl
from jax.experimental.pallas import tpu as pltpu
from jax.sharding import PartitionSpec as P

HEAD_WIDTH = 128
PAGE_POSITIONS = 128
MAX_SLOT_PAGES = 15
GROUP = 8
SUBGROUP = 2
LANES = 128
PAIRS = 32
SCALE = HEAD_WIDTH ** (-0.5)
NT = (((1,), (1,)), ((), ()))
NEG = float("-inf")
MESH = pl.DeviceIdType.MESH
F32, BF16, I32 = jnp.float32, jnp.bfloat16, jnp.int32


def iota(shape, dim):
    return lax.broadcasted_iota(I32, shape, dim)


def remote(src, dst, send_sem, recv_sem, axis, peer):
    return pltpu.make_async_remote_copy(
        src_ref=src,
        dst_ref=dst,
        send_sem=send_sem,
        recv_sem=recv_sem,
        device_id={axis: peer},
        device_id_type=MESH,
    )


def segment_scan(x, at, lane, width, combine, empty):
    ahead, behind = x, x
    shift = 1
    while shift < MAX_SLOT_PAGES:
        same = (pltpu.roll(at, shift, 1) == at) & (lane >= shift)
        ahead = combine(ahead, jnp.where(same, pltpu.roll(ahead, shift, 1), empty))
        same = (pltpu.roll(at, width - shift, 1) == at) & (lane < width - shift)
        behind = combine(behind, jnp.where(same, pltpu.roll(behind, width - shift, 1), empty))
        shift *= 2
    return ahead, behind


def pick(mask, row, axis):
    return jnp.sum(jnp.where(mask, row, 0.0), axis=axis, keepdims=True)


def page_tables(me, rows, extra, pages, entries, home_cap, home, pieces, lengths):
    batch, jobs = home.shape[1], pieces.shape[1]
    lengths = lengths.astype(F32)
    piece_req, piece_len = pieces[0:1].astype(F32), pieces[1:2].astype(F32)
    lane = iota((rows, batch), 1)
    mine = iota((rows, batch), 0) + me * rows
    hot = home == mine
    home_req = pick(hot, lane.astype(F32), 1)
    home_len = pick(hot, lengths, 1) - pick(piece_req == home_req, piece_len, 1)
    hot = iota((extra, jobs), 1) == iota((extra, jobs), 0) + me * extra
    guest_req, guest_len = pick(hot, piece_req, 1), pick(hot, piece_len, 1)
    count = -(-(rows + extra) // LANES) * LANES
    spare = count - rows - extra
    request = jnp.concatenate([home_req, guest_req, jnp.full((spare, 1), -1.0, F32)], axis=0)
    length = jnp.concatenate([home_len, guest_len, jnp.zeros((spare, 1), F32)], axis=0)
    held_pages = jnp.floor((length + (PAGE_POSITIONS - 1)) * (1.0 / PAGE_POSITIONS))
    device = jnp.floor((request + 0.5) * (1.0 / rows))
    column = iota((count, LANES), 1)
    turned = jnp.where(column == 0, device, jnp.where(column == 1, held_pages, 0.0)).T
    slot, other = iota((count, count), 0), iota((count, count), 1)
    before = other < slot
    alike = jnp.where(slot < rows, 1, 0) == jnp.where(other < rows, 1, 0)
    rank = pick(before & alike & (turned[0:1] == device), 1.0, 1)
    begin = pick(before, turned[1:2], 1)
    guest = jnp.where(iota((count, 1), 0) < rows, 0.0, float(home_cap))
    entry = device * entries + guest + rank
    page = iota((count, pages), 1).astype(F32)
    held = (begin <= page) & (page < begin + held_pages)
    left = jnp.clip(length - (page - begin) * PAGE_POSITIONS, 0.0, float(PAGE_POSITIONS))
    page_entry = pick(held, entry, 0)
    page_request = pick(held, request, 0)
    page_row = pick(held, request - device * rows + 1.0, 0)
    page_used = pick(held, left, 0)
    return page_entry, page_request, page_row, page_used


def kernel(
    n, kv, entries, home_cap,
    home_ref, pieces_ref, lengths_ref, latest_ref, query_ref, cache_ref, weight_ref, out_ref,
    keys, values, weight, q_all, q_buf, o_buf, used_buf, top_buf, sum_buf, hot_in, hot_out,
    slots, got, stat_out, stat_got, merge, attended, terms, own_term, z_out, z_in,
    load_sem, q_send, q_recv, s_send, s_recv, z_send, z_recv,
):
    me, pos = lax.axis_index("req"), lax.axis_index("kv")
    rows, width = query_ref.shape
    extra = pieces_ref.shape[1] // n
    pages = cache_ref.shape[1] // PAGE_POSITIONS
    total = n * entries
    groups = GROUP // SUBGROUP
    out_width = weight_ref.shape[1] // kv
    half = out_width // 2

    own_query = pltpu.make_async_copy(query_ref, q_all.at[me], load_sem.at[0])
    load_keys = pltpu.make_async_copy(cache_ref.at[0], keys, load_sem.at[1])
    load_values = pltpu.make_async_copy(cache_ref.at[1], values, load_sem.at[2])
    load_weight = pltpu.make_async_copy(weight_ref, weight, load_sem.at[3])
    own_query.start()
    load_keys.start()
    load_values.start()
    load_weight.start()

    barrier = pltpu.get_barrier_semaphore()
    for step in range(1, n):
        pl.semaphore_signal(
            barrier, inc=1, device_id={"req": lax.rem(me + step, n)}, device_id_type=MESH
        )

    @pl.when(pos > 0)
    def _():
        pl.semaphore_signal(barrier, inc=1, device_id={"kv": pos - 1}, device_id_type=MESH)

    @pl.when(pos < kv - 1)
    def _():
        pl.semaphore_signal(barrier, inc=1, device_id={"kv": pos + 1}, device_id_type=MESH)

    neighbours = (pos + kv - 1) // kv + (2 * kv - 2 - pos) // kv
    pl.semaphore_wait(barrier, n - 1 + neighbours)
    own_query.wait()

    def hand(owner, part, parts, sem, peer):
        size = rows // parts
        block = q_all.at[owner, part * size : (part + 1) * size]
        return remote(block, block, q_send.at[sem], q_recv.at[sem], "req", me ^ peer)

    sent = []

    def begin(copy):
        copy.start()
        sent.append(copy)

    begin(hand(me, 0, 1, 0, 1))
    if n == 8:
        first = [hand(me, 0, 2, 1, 2), hand(me, 1, 2, 2, 4), hand(me, 1, 2, 3, 2), hand(me, 0, 2, 4, 4)]
    else:
        first = [hand(me, 0, 1, k, k) for k in range(2, n, 2)]
    for copy in first:
        begin(copy)

    page_entry, page_request, page_row, page_used = page_tables(
        me, rows, extra, pages, entries, home_cap,
        home_ref[...], pieces_ref[...], lengths_ref[...],
    )
    line = iota((LANES, pages), 0)
    turned = jnp.where(line == 0, page_request, jnp.where(line == 1, page_used, 0.0)).T
    hot = turned[:, 0:1].astype(I32) == iota((pages, n * rows), 1)
    hot_in[...] = jnp.where(hot, 1.0, 0.0).astype(BF16)
    used = jnp.broadcast_to(turned[:, 1:2], (pages, LANES))
    for h in range(GROUP):
        used_buf[pl.ds(h, pages, stride=GROUP), :] = used
    hot = page_entry.astype(I32) == iota((total, pages), 0)
    hot_out[...] = jnp.where(hot, 1.0, 0.0).astype(BF16)

    if n == 8:
        first[0].wait_recv()
        begin(hand(me ^ 2, 0, 2, 5, 4))
        begin(hand(me ^ 2, 0, 2, 7, 1))
        first[1].wait_recv()
        begin(hand(me ^ 4, 1, 2, 6, 2))
        begin(hand(me ^ 4, 1, 2, 8, 1))
        first[2].wait_recv()
        begin(hand(me ^ 2, 1, 2, 9, 1))
        first[3].wait_recv()
        begin(hand(me ^ 4, 0, 2, 10, 1))
        hand(me ^ 6, 0, 2, 5, 4).wait_recv()
        begin(hand(me ^ 6, 0, 2, 11, 1))
        hand(me ^ 6, 1, 2, 6, 2).wait_recv()
        begin(hand(me ^ 6, 1, 2, 12, 1))
        hand(me ^ 1, 0, 1, 0, 1).wait_recv()
        for sem, owner, part in ((7, 3, 0), (8, 5, 1), (9, 3, 1), (10, 5, 0), (11, 7, 0), (12, 7, 1)):
            hand(me ^ owner, part, 2, sem, 1).wait_recv()
    else:
        for k in range(2, n, 2):
            first[k // 2 - 1].wait_recv()
            begin(hand(me ^ k, 0, 1, k + 1, 1))
        hand(me ^ 1, 0, 1, 0, 1).wait_recv()
        for k in range(2, n, 2):
            hand(me ^ k ^ 1, 0, 1, k + 1, 1).wait_recv()

    everyone = q_all[...].reshape(n * rows, width)
    for h in range(GROUP):
        q_buf[pl.ds(h, pages, stride=GROUP), :] = jnp.dot(
            hot_in[...],
            everyone[:, h * HEAD_WIDTH : (h + 1) * HEAD_WIDTH],
            preferred_element_type=F32,
        )
    load_keys.wait()
    load_values.wait()

    pair = 2 * GROUP
    span = 2 * PAGE_POSITIONS
    lane = iota((GROUP, LANES), 1)
    column = iota((pair, LANES), 1).astype(F32)
    upper = iota((pair, LANES), 0) < GROUP
    left_column = jnp.where(upper, column, 2.0 * span)
    right_column = jnp.where(upper, 2.0 * span, column)
    limit = jnp.concatenate([left_column, right_column], axis=1)
    ones = jnp.ones((span, LANES), BF16)
    per_chunk = LANES // (2 * PAIRS)

    def attend(step, carry):
        chunk = step // per_chunk
        lane0 = (step - chunk * per_chunk) * (2 * PAIRS)
        row0 = pl.multiple_of(step * (PAIRS * pair), PAIRS * pair)
        key0 = pl.multiple_of(step * (PAIRS * span), PAIRS * span)
        tops, sums = top_buf[chunk], sum_buf[chunk]
        scores = []
        for j in range(PAIRS):
            q = q_buf[pl.ds(row0 + j * pair, pair), :].astype(BF16)
            block = keys[pl.ds(key0 + j * span, span), :]
            scores.append(lax.dot_general(q, block, NT, preferred_element_type=F32))
        weights = []
        for j in range(PAIRS):
            filled = used_buf[pl.ds(row0 + j * pair, pair), :]
            in_use = limit < jnp.concatenate([filled, filled], axis=1)
            s = jnp.where(in_use, scores[j] * SCALE, NEG)
            top = jnp.max(s, axis=1, keepdims=True)
            weights.append(jnp.exp(s - top).astype(BF16))
            for k in range(2):
                here = lane == lane0 + 2 * j + k
                tops = jnp.where(here, top[k * GROUP : (k + 1) * GROUP], tops)
        totals = jnp.dot(jnp.concatenate(weights, axis=0), ones, preferred_element_type=F32)
        for p in range(2 * PAIRS):
            sums = jnp.where(lane == lane0 + p, totals[p * GROUP : (p + 1) * GROUP], sums)
        for j in range(PAIRS):
            block = values[pl.ds(key0 + j * span, span), :]
            o_buf[pl.ds(row0 + j * pair, pair), :] = jnp.dot(
                weights[j], block, preferred_element_type=F32
            )
        top_buf[chunk] = tops
        sum_buf[chunk] = sums
        return carry

    top_buf[...] = jnp.zeros_like(top_buf)
    sum_buf[...] = jnp.zeros_like(sum_buf)
    lax.fori_loop(0, pages // (2 * PAIRS), attend, 0)

    chunks = pages // LANES
    top = jnp.concatenate([top_buf[c] for c in range(chunks)], axis=1)
    page_sum = jnp.concatenate([sum_buf[c] for c in range(chunks)], axis=1)
    at = jnp.broadcast_to(page_entry, (GROUP, pages))
    where = iota((GROUP, pages), 1)
    ahead, behind = segment_scan(top, at, where, pages, jnp.maximum, NEG)
    slot_top = jnp.maximum(ahead, behind)
    factor = jnp.exp(top - slot_top)
    part = page_sum * factor
    ahead, behind = segment_scan(part, at, where, pages, jnp.add, 0.0)
    slot_sum = jnp.maximum(ahead + behind - part, part)
    lse = slot_top + jnp.log(slot_sum)
    start = (where == 0) | (pltpu.roll(at, 1, 1) != at)
    start = jnp.where(start, 1.0, 0.0)
    high = lse.astype(BF16).astype(F32)
    rest = lse - high
    middle = rest.astype(BF16).astype(F32)
    low = rest - middle
    number = jnp.broadcast_to(page_row, (GROUP, pages))
    stacked = jnp.concatenate(
        [high * start, middle * start, low * start, number * start], axis=0
    ).astype(BF16)
    placed = lax.dot_general(stacked, hot_out[...], NT, preferred_element_type=F32)
    placed = jnp.concatenate(
        [
            placed[:GROUP] + placed[GROUP : 2 * GROUP] + placed[2 * GROUP : 3 * GROUP],
            placed[3 * GROUP :],
        ],
        axis=0,
    )
    column = iota((2 * GROUP, LANES), 1)
    for d in range(n):
        piece = placed if d == 0 else pltpu.roll(placed, total - d * entries, 1)
        stat_out[d] = jnp.where(column < entries, piece[:, :LANES], 0.0)

    def ship(source, target, index):
        copies = []
        for step in range(1, n):
            peer = lax.rem(me + step, n)
            copy = remote(
                source.at[peer], target.at[me],
                s_send.at[index, step], s_recv.at[index, step], "req", peer,
            )
            copy.start()
            copies.append(copy)
        target[me] = source[me]
        return copies

    stat_copies = ship(stat_out, stat_got, groups)
    ratio = jnp.concatenate(
        [factor / slot_sum, jnp.zeros((LANES - GROUP, pages), F32)], axis=0
    ).T
    slot_copies = []
    for g in range(groups):
        block = jnp.concatenate(
            [
                (o_buf[pl.ds(h, pages, stride=GROUP), :] * ratio[:, h : h + 1]).astype(BF16)
                for h in range(g * SUBGROUP, (g + 1) * SUBGROUP)
            ],
            axis=1,
        )
        block = jnp.dot(hot_out[...], block, preferred_element_type=F32).astype(BF16)
        slots[g] = block.reshape(n, entries, SUBGROUP * HEAD_WIDTH)
        slot_copies.append(ship(slots.at[g], got.at[g], g))

    own_q = q_all[me].astype(F32)
    latest_key = latest_ref[0].astype(F32)
    latest_value = latest_ref[1].astype(F32)
    selfs = []
    for h in range(GROUP):
        q = own_q[:, h * HEAD_WIDTH : (h + 1) * HEAD_WIDTH]
        selfs.append(jnp.sum(q * latest_key, axis=1, keepdims=True) * SCALE)
    for copy in stat_copies:
        copy.wait()
    stats = jnp.zeros((2 * GROUP, total), F32)
    for s in range(n):
        piece = jnp.concatenate(
            [stat_got[s], jnp.zeros((2 * GROUP, total - LANES), F32)], axis=1
        )
        stats = stats + (piece if s == 0 else pltpu.roll(piece, s * entries, 1))
    mine = stats[GROUP : GROUP + 1].astype(I32) == iota((rows, total), 0) + 1
    own_weights = []
    for h in range(GROUP):
        score = jnp.where(mine, stats[h : h + 1], NEG)
        top = jnp.maximum(jnp.max(score, axis=1, keepdims=True), selfs[h])
        w = jnp.exp(score - top)
        own = jnp.exp(selfs[h] - top)
        denominator = jnp.sum(w, axis=1, keepdims=True) + own
        w = w / denominator
        high = w.astype(BF16)
        merge[h, :rows] = high
        merge[h, rows:] = (w - high.astype(F32)).astype(BF16)
        own_weights.append(own / denominator)
    for g in range(groups):
        for copy in slot_copies[g]:
            copy.wait()
        block = got[g].reshape(total, SUBGROUP * HEAD_WIDTH)
        for k in range(SUBGROUP):
            h = g * SUBGROUP + k
            both = jnp.dot(
                merge[h],
                block[:, k * HEAD_WIDTH : (k + 1) * HEAD_WIDTH],
                preferred_element_type=F32,
            )
            result = both[:rows] + both[rows:] + latest_value * own_weights[h]
            attended[:, h * HEAD_WIDTH : (h + 1) * HEAD_WIDTH] = result.astype(BF16)
    load_weight.wait()

    def project(offset):
        return jnp.dot(attended[...], weight[:, pl.ds(offset, half)], preferred_element_type=F32)

    def pass_on(way, block, f, source=None):
        return remote(
            z_out.at[way, block, f],
            z_in.at[way, block, f],
            z_send.at[way, block, f],
            z_recv.at[way, block, f],
            "kv",
            pos + 1 if way == 0 else pos - 1,
        )

    order = []
    for k in range(kv - 1):
        order += [(0, kv - 1 - k, f) for f in range(2)] + [(1, k, f) for f in range(2)]

    for way, block, f in order:
        ahead = pos < block if way == 0 else pos > block
        edge = pos == 0 if way == 0 else pos == kv - 1

        @pl.when(edge)
        def _():
            z_out[way, block, f] = project(block * out_width + f * half).astype(BF16)
            pass_on(way, block, f).start()

        @pl.when(ahead & jnp.logical_not(edge))
        def _():
            terms[block, f] = project(block * out_width + f * half)

    for f in range(2):
        own_term[f] = project(pl.multiple_of(pos * out_width + f * half, half))

    for place in range(kv):

        @pl.when(pos == place)
        def _():
            relays = []
            for way, block, f in order:
                ahead = place < block if way == 0 else place > block
                hops = place if way == 0 else kv - 1 - place
                turn = (kv - 1 - block if way == 0 else block) * 2 + f
                if ahead and hops:
                    relays.append((2 * turn + 4 * hops, way, block, f))
            for _, way, block, f in sorted(relays):
                pass_on(way, block, f).wait_recv()
                z_out[way, block, f] = (terms[block, f] + z_in[way, block, f].astype(F32)).astype(BF16)
                pass_on(way, block, f).start()
            for f in range(2):
                result = own_term[f]
                for way in range(2):
                    if (place if way == 0 else kv - 1 - place) > 0:
                        pass_on(way, place, f).wait_recv()
                        result = result + z_in[way, place, f].astype(F32)
                out_ref[:, f * half : (f + 1) * half] = result.astype(BF16)
            for way, block, f in order:
                if place < block if way == 0 else place > block:
                    pass_on(way, block, f).wait_send()

    for copy in sent:
        copy.wait_send()


def per_device(query, latest_key_value, cache, out_weight, home, pieces, lengths):
    n = lax.axis_size("req")
    kv = lax.axis_size("kv")
    rows, width = query.shape
    extra = pieces.shape[1] // n
    batch = home.shape[0]
    positions = cache.shape[1]
    pages = positions // PAGE_POSITIONS
    home_cap = 2 * rows // n
    entries = -(-(home_cap + 2 * extra // n) // 16) * 16
    total = n * entries
    groups = GROUP // SUBGROUP
    out_width = out_weight.shape[1] // kv
    half = out_width // 2
    vmem = pl.BlockSpec(memory_space=pltpu.VMEM)
    anywhere = pl.BlockSpec(memory_space=pl.ANY)
    dma = pltpu.SemaphoreType.DMA
    buffer = pltpu.VMEM
    return pl.pallas_call(
        functools.partial(kernel, n, kv, entries, home_cap),
        name="paged_decode",
        out_shape=jax.ShapeDtypeStruct((rows, out_width), BF16),
        in_specs=[vmem, vmem, vmem, vmem, anywhere, anywhere, anywhere],
        out_specs=vmem,
        scratch_shapes=[
            buffer((positions, HEAD_WIDTH), BF16),
            buffer((positions, HEAD_WIDTH), BF16),
            buffer(out_weight.shape, BF16),
            buffer((n, rows, width), BF16),
            buffer((pages * GROUP, HEAD_WIDTH), F32),
            buffer((pages * GROUP, HEAD_WIDTH), F32),
            buffer((pages * GROUP, LANES), F32),
            buffer((pages // LANES, GROUP, LANES), F32),
            buffer((pages // LANES, GROUP, LANES), F32),
            buffer((pages, n * rows), BF16),
            buffer((total, pages), BF16),
            buffer((groups, n, entries, SUBGROUP * HEAD_WIDTH), BF16),
            buffer((groups, n, entries, SUBGROUP * HEAD_WIDTH), BF16),
            buffer((n, 2 * GROUP, LANES), F32),
            buffer((n, 2 * GROUP, LANES), F32),
            buffer((GROUP, 2 * rows, total), BF16),
            buffer((rows, width), BF16),
            buffer((kv, 2, rows, half), F32),
            buffer((2, rows, half), F32),
            buffer((2, kv, 2, rows, half), BF16),
            buffer((2, kv, 2, rows, half), BF16),
            dma((4,)),
            dma((max(13, n),)),
            dma((max(13, n),)),
            dma((groups + 1, n)),
            dma((groups + 1, n)),
            dma((2, kv, 2)),
            dma((2, kv, 2)),
        ],
        compiler_params=pltpu.CompilerParams(
            collective_id=1, has_side_effects=True, vmem_limit_bytes=60 << 20
        ),
    )(
        home.reshape(1, batch),
        pieces,
        lengths.reshape(1, batch),
        latest_key_value,
        query,
        cache,
        out_weight,
    )


def solution(mesh):
    placed = (
        P("req", "kv"),
        P(None, "req", "kv"),
        P(None, "req", "kv"),
        P("kv", None),
        P(),
        P(),
        P(),
    )
    return jax.shard_map(
        per_device, mesh=mesh, in_specs=placed, out_specs=P("req", "kv"), check_vma=False
    )
```

```python
import functools

import jax
import jax.numpy as jnp
from jax import lax
from jax.experimental import pallas as pl
from jax.experimental.pallas import tpu as pltpu
from jax.sharding import PartitionSpec as P

HEAD_WIDTH = 128
PAGE_POSITIONS = 128
MAX_SLOT_PAGES = 15
GROUP = 8
SUBGROUP = 2
LANES = 128
PAIRS = 64
CHUNK = 32
SCALE = HEAD_WIDTH ** (-0.5)
NT = (((1,), (1,)), ((), ()))
NEG = float("-inf")
MESH = pl.DeviceIdType.MESH
F32, BF16, I32 = jnp.float32, jnp.bfloat16, jnp.int32


def iota(shape, dim):
    return lax.broadcasted_iota(I32, shape, dim)


def remote(src, dst, send_sem, recv_sem, axis, peer):
    return pltpu.make_async_remote_copy(
        src_ref=src,
        dst_ref=dst,
        send_sem=send_sem,
        recv_sem=recv_sem,
        device_id={axis: peer},
        device_id_type=MESH,
    )


def segment_scan(x, at, lane, width, combine, empty):
    ahead, behind = x, x
    shift = 1
    while shift < MAX_SLOT_PAGES:
        same = (pltpu.roll(at, shift, 1) == at) & (lane >= shift)
        ahead = combine(ahead, jnp.where(same, pltpu.roll(ahead, shift, 1), empty))
        same = (pltpu.roll(at, width - shift, 1) == at) & (lane < width - shift)
        behind = combine(behind, jnp.where(same, pltpu.roll(behind, width - shift, 1), empty))
        shift *= 2
    return ahead, behind


def pick(mask, row, axis):
    return jnp.sum(jnp.where(mask, row, 0.0), axis=axis, keepdims=True)


def page_tables(me, rows, extra, pages, plan, home, pieces, lengths):
    n, entries, early, guest_cap, early_homes, early_rows = plan
    batch, jobs = home.shape[1], pieces.shape[1]
    home_f, lengths = home.astype(F32), lengths.astype(F32)
    piece_req, piece_len = pieces[0:1].astype(F32), pieces[1:2].astype(F32)
    lane = iota((rows, batch), 1)
    mine = iota((rows, batch), 0) + me * rows
    my_home = pick(lane == mine, home_f, 1)
    hot = home == mine
    home_req = pick(hot, lane.astype(F32), 1)
    home_len = pick(hot, lengths, 1) - pick(piece_req == home_req, piece_len, 1)
    hot = iota((extra, jobs), 1) == iota((extra, jobs), 0) + me * extra
    guest_req, guest_len = pick(hot, piece_req, 1), pick(hot, piece_len, 1)
    count = -(-(rows + extra) // LANES) * LANES
    spare = count - rows - extra
    request = jnp.concatenate([home_req, guest_req, jnp.full((spare, 1), -1.0, F32)], axis=0)
    length = jnp.concatenate([home_len, guest_len, jnp.zeros((spare, 1), F32)], axis=0)
    my_home = jnp.concatenate([my_home, jnp.full((count - rows, 1), -1.0, F32)], axis=0)
    held_pages = jnp.floor((length + (PAGE_POSITIONS - 1)) * (1.0 / PAGE_POSITIONS))
    device = jnp.floor((request + 0.5) * (1.0 / rows))
    column = iota((count, LANES), 1)
    turned = jnp.where(column == 1, held_pages, jnp.where(column == 2, my_home, 0.0))
    turned = jnp.where(column == 0, device, turned).T
    slot, other = iota((count, count), 0), iota((count, count), 1)
    before = other < slot
    alike = jnp.where(slot < rows, 1, 0) == jnp.where(other < rows, 1, 0)
    rank = pick(before & alike & (turned[0:1] == device), 1.0, 1)
    begin = pick(before, turned[1:2], 1)
    rank = rank + jnp.where(iota((count, 1), 0) < rows, float(guest_cap), 0.0)
    late = n * early + device * (entries - early) + rank - early
    entry = jnp.where(rank < early, device * early + rank, late)
    page = iota((count, pages), 1).astype(F32)
    held = (begin <= page) & (page < begin + held_pages)
    left = jnp.clip(length - (page - begin) * PAGE_POSITIONS, 0.0, float(PAGE_POSITIONS))
    page_entry = pick(held, entry, 0)
    page_request = pick(held, request, 0)
    page_row = pick(held, request - device * rows + 1.0, 0)
    page_used = pick(held, left, 0)

    at_c, at_r = my_home[:LANES], turned[2:3, :LANES]
    owner_c = jnp.floor((at_c + 0.5) * (1.0 / rows))
    owner_r = jnp.floor((at_r + 0.5) * (1.0 / rows))
    sub, lane = iota((LANES, LANES), 0), iota((LANES, LANES), 1)
    same = owner_c == owner_r
    late_c = jnp.where(pick(same & (at_r < at_c), 1.0, 1) < early_homes, 0.0, 1.0)
    late_r = jnp.where(pick(same & (at_c < at_r), 1.0, 0) < early_homes, 0.0, 1.0)
    same = late_c == late_r
    turn_c = pick(same & (lane < sub), 1.0, 1) + late_c * early_rows
    turn_r = pick(same & (sub < lane), 1.0, 0) + late_r * early_rows
    there = (turn_r == sub.astype(F32)) & (lane < rows)
    there = jnp.where(there, 1.0, 0.0)[:rows]
    back = jnp.where(turn_c == lane.astype(F32), 1.0, 0.0)[:rows]
    merged = pick(there > 0.5, lane[:rows].astype(F32) + 1.0, 1)
    return page_entry, page_request, page_row, page_used, there, back, merged


def kernel(
    n, kv, plan,
    home_hbm, pieces_hbm, lengths_hbm, latest_hbm, query_hbm, cache_hbm, weight_hbm, out_ref,
    home, pieces, lengths, latest, keys, values, weight, q_all, q_buf, o_buf, used_buf,
    top_buf, sum_buf, hot_in, hot_out, there, back, early_out, early_in, late_out, late_in,
    stat_out, stat_in, early_merge, late_merge, attended, terms, own_term, final, z_out, z_in,
    load_sem, q_send, q_recv, s_send, s_recv, z_send, z_recv,
):
    me, pos = lax.axis_index("req"), lax.axis_index("kv")
    _, entries, early, _, _, early_rows = plan
    rows, width = query_hbm.shape
    extra = pieces.shape[1] // n
    pages = cache_hbm.shape[1] // PAGE_POSITIONS
    total, first_total = n * entries, n * early
    late = entries - early
    groups = GROUP // SUBGROUP
    out_width = weight.shape[1] // kv
    half = out_width // 2

    barrier = pltpu.get_barrier_semaphore()
    for step in range(1, n):
        pl.semaphore_signal(barrier, inc=1, device_id={"req": me ^ step}, device_id_type=MESH)

    for step in (1, 2):
        pl.semaphore_signal(barrier, inc=1, device_id={"kv": pos ^ step}, device_id_type=MESH)
    inner = (pos + 1) // 2 % 2

    @pl.when(inner == 1)
    def _():
        pl.semaphore_signal(barrier, inc=1, device_id={"kv": pos ^ 3}, device_id_type=MESH)

    loads = [
        pltpu.make_async_copy(source, target, load_sem.at[i])
        for i, (source, target) in enumerate(
            [
                (query_hbm, q_all.at[0]),
                (home_hbm, home),
                (pieces_hbm, pieces),
                (lengths_hbm, lengths),
                (latest_hbm, latest),
                (cache_hbm.at[0], keys),
                (cache_hbm.at[1], values),
                (weight_hbm, weight),
            ]
        )
    ]
    for load in loads:
        load.start()
    loads[0].wait()
    pl.semaphore_wait(barrier, n + 1 + inner)

    def hand(block, part, parts, sem, peer):
        size = rows // parts
        span = slice(part * size, (part + 1) * size)
        return remote(
            q_all.at[block, span], q_all.at[block ^ peer, span],
            q_send.at[sem], q_recv.at[sem], "req", me ^ peer,
        )

    sent = []

    def begin(copy):
        copy.start()
        sent.append(copy)

    if n == 8:
        first = [hand(0, 0, 2, 1, 2), hand(0, 1, 2, 2, 4), hand(0, 1, 2, 3, 2), hand(0, 0, 2, 4, 4)]
    else:
        first = [hand(0, 0, 1, k, k) for k in range(2, n, 2)]
    for copy in first:
        begin(copy)
    sibling = hand(0, 0, 1, 0, 1)
    begin(sibling)

    for load in loads[1:5]:
        load.wait()
    page_entry, page_request, page_row, page_used, there_v, back_v, merged = page_tables(
        me, rows, extra, pages, plan,
        home[...].reshape(1, -1), pieces[...], lengths[...].reshape(1, -1),
    )
    there[...] = there_v.astype(BF16)
    back[...] = back_v.astype(BF16)
    line = iota((LANES, pages), 0)
    turned = jnp.where(line == 0, page_request, jnp.where(line == 1, page_used, 0.0)).T
    asked = turned[:, 0:1]
    owner = jnp.floor((asked + 0.5) * (1.0 / rows))
    place = asked.astype(I32) - owner.astype(I32) * rows + (owner.astype(I32) ^ me) * rows
    hot = place == iota((pages, n * rows), 1)
    hot_in[...] = jnp.where(hot, 1.0, 0.0).astype(BF16)
    used = jnp.broadcast_to(turned[:, 1:2], (pages, LANES))
    for h in range(GROUP):
        used_buf[pl.ds(h, pages, stride=GROUP), :] = used
    hot = page_entry.astype(I32) == iota((total, pages), 0)
    hot_out[...] = jnp.where(hot, 1.0, 0.0).astype(BF16)

    def gather(start, stop, more):
        block = q_all[start:stop].reshape((stop - start) * rows, width)
        hot = hot_in[:, start * rows : stop * rows]
        for h in range(GROUP):
            at = pl.ds(h, pages, stride=GROUP)
            q = jnp.dot(
                hot, block[:, h * HEAD_WIDTH : (h + 1) * HEAD_WIDTH], preferred_element_type=F32
            )
            q_buf[at, :] = q_buf[at, :] + q if more else q

    if n == 8:
        first[0].wait_recv()
        begin(hand(2, 0, 2, 5, 4))
        begin(hand(2, 0, 2, 7, 1))
        first[1].wait_recv()
        begin(hand(4, 1, 2, 6, 2))
        begin(hand(4, 1, 2, 8, 1))
        first[2].wait_recv()
        begin(hand(2, 1, 2, 9, 1))
        first[3].wait_recv()
        begin(hand(4, 0, 2, 10, 1))
        sibling.wait_recv()
        for sem, block, part in ((7, 2, 0), (8, 4, 1), (9, 2, 1), (10, 4, 0)):
            hand(block, part, 2, sem, 1).wait_recv()
        gather(0, 6, False)
        hand(2, 0, 2, 5, 4).wait_recv()
        begin(hand(6, 0, 2, 11, 1))
        hand(4, 1, 2, 6, 2).wait_recv()
        begin(hand(6, 1, 2, 12, 1))
        for sem, part in ((11, 0), (12, 1)):
            hand(6, part, 2, sem, 1).wait_recv()
        gather(6, 8, True)
    else:
        for k in range(2, n, 2):
            first[k // 2 - 1].wait_recv()
            begin(hand(k, 0, 1, k + 1, 1))
        sibling.wait_recv()
        for k in range(2, n, 2):
            hand(k, 0, 1, k + 1, 1).wait_recv()
        gather(0, n, False)
    loads[5].wait()
    loads[6].wait()

    pair = 2 * GROUP
    span = 2 * PAGE_POSITIONS
    lane = iota((GROUP, LANES), 1)
    column = iota((pair, LANES), 1).astype(F32)
    upper = iota((pair, LANES), 0) < GROUP
    left_column = jnp.where(upper, column, 2.0 * span)
    right_column = jnp.where(upper, 2.0 * span, column)
    limit = jnp.concatenate([left_column, right_column], axis=1)
    ones = jnp.ones((span, LANES), BF16)

    def attend(chunk, carry):
        row0 = pl.multiple_of(chunk * (PAIRS * pair), PAIRS * pair)
        key0 = pl.multiple_of(chunk * (PAIRS * span), PAIRS * span)
        tops = jnp.zeros((GROUP, LANES), F32)
        sums = jnp.zeros((GROUP, LANES), F32)
        scores = []
        for j in range(PAIRS):
            q = q_buf[pl.ds(row0 + j * pair, pair), :].astype(BF16)
            block = keys[pl.ds(key0 + j * span, span), :]
            scores.append(lax.dot_general(q, block, NT, preferred_element_type=F32))
        weights = []
        for j in range(PAIRS):
            filled = used_buf[pl.ds(row0 + j * pair, pair), :]
            in_use = limit < jnp.concatenate([filled, filled], axis=1)
            s = jnp.where(in_use, scores[j] * SCALE, NEG)
            top = jnp.max(s, axis=1, keepdims=True)
            weights.append(jnp.exp(s - top).astype(BF16))
            for k in range(2):
                tops = jnp.where(lane == 2 * j + k, top[k * GROUP : (k + 1) * GROUP], tops)
        totals = jnp.dot(jnp.concatenate(weights, axis=0), ones, preferred_element_type=F32)
        for p in range(2 * PAIRS):
            sums = jnp.where(lane == p, totals[p * GROUP : (p + 1) * GROUP], sums)
        for j in range(PAIRS):
            block = values[pl.ds(key0 + j * span, span), :]
            o_buf[pl.ds(row0 + j * pair, pair), :] = jnp.dot(
                weights[j], block, preferred_element_type=F32
            )
        top_buf[chunk] = tops
        sum_buf[chunk] = sums
        return carry

    lax.fori_loop(0, pages // (2 * PAIRS), attend, 0)

    chunks = pages // LANES
    top = jnp.concatenate([top_buf[c] for c in range(chunks)], axis=1)
    page_sum = jnp.concatenate([sum_buf[c] for c in range(chunks)], axis=1)
    at = jnp.broadcast_to(page_entry, (GROUP, pages))
    where = iota((GROUP, pages), 1)
    ahead, behind = segment_scan(top, at, where, pages, jnp.maximum, NEG)
    slot_top = jnp.maximum(ahead, behind)
    factor = jnp.exp(top - slot_top)
    part = page_sum * factor
    ahead, behind = segment_scan(part, at, where, pages, jnp.add, 0.0)
    slot_sum = jnp.maximum(ahead + behind - part, part)
    lse = slot_top + jnp.log(slot_sum)
    start = (where == 0) | (pltpu.roll(at, 1, 1) != at)
    start = jnp.where(start, 1.0, 0.0)
    high = lse.astype(BF16).astype(F32)
    rest = lse - high
    middle = rest.astype(BF16).astype(F32)
    low = rest - middle
    number = jnp.broadcast_to(page_row, (GROUP, pages))
    stacked = jnp.concatenate(
        [high * start, middle * start, low * start, number * start], axis=0
    ).astype(BF16)
    placed = lax.dot_general(stacked, hot_out[...], NT, preferred_element_type=F32)
    placed = jnp.concatenate(
        [
            placed[:GROUP] + placed[GROUP : 2 * GROUP] + placed[2 * GROUP : 3 * GROUP],
            placed[3 * GROUP :],
        ],
        axis=0,
    )
    column = iota((2 * GROUP, LANES), 1)

    def turn(x, by):
        by = by % total
        return pltpu.roll(x, by, 1) if by else x

    for b in range(n):
        piece = jnp.where(column < early, turn(placed, -b * early)[:, :LANES], 0.0)
        if late:
            other = turn(placed, early - first_total - b * late)[:, :LANES]
            piece = jnp.where((column >= early) & (column < entries), other, piece)
        stat_out[b] = piece

    def ship(source, target, index):
        copies = []
        for step in range(1, n):
            peer = lax.rem(me + step, n)
            copy = remote(
                source.at[peer], target.at[me],
                s_send.at[index, step], s_recv.at[index, step], "req", peer,
            )
            copy.start()
            copies.append(copy)
        target[me] = source[me]
        return copies

    stat_copies = ship(stat_out, stat_in, groups)
    ratio = jnp.concatenate(
        [factor / slot_sum, jnp.zeros((LANES - GROUP, pages), F32)], axis=0
    ).T
    slot_copies = []
    wide = SUBGROUP * HEAD_WIDTH
    for g in range(groups):
        block = jnp.concatenate(
            [
                (o_buf[pl.ds(h, pages, stride=GROUP), :] * ratio[:, h : h + 1]).astype(BF16)
                for h in range(g * SUBGROUP, (g + 1) * SUBGROUP)
            ],
            axis=1,
        )
        block = jnp.dot(hot_out[...], block, preferred_element_type=F32).astype(BF16)
        early_out[g] = block[:first_total].reshape(n, early, wide)
        slot_copies.append(ship(early_out.at[g], early_in.at[g], g))
        if late:
            late_out[:, :, g * wide : (g + 1) * wide] = block[first_total:].reshape(n, late, wide)
    if late:
        late_copies = ship(late_out, late_in, groups + 1)

    own_q = jnp.dot(there[:, :rows], q_all[0], preferred_element_type=F32)
    latest_key = jnp.dot(there[:, :rows], latest[0], preferred_element_type=F32)
    latest_value = jnp.dot(there[:, :rows], latest[1], preferred_element_type=F32)
    selfs = []
    for h in range(GROUP):
        q = own_q[:, h * HEAD_WIDTH : (h + 1) * HEAD_WIDTH]
        selfs.append(jnp.sum(q * latest_key, axis=1, keepdims=True) * SCALE)
    for copy in stat_copies:
        copy.wait()
    stats = jnp.zeros((2 * GROUP, total), F32)
    for s in range(n):
        got = stat_in[s]
        piece = jnp.where(column < early, got, 0.0)
        spare = jnp.zeros((2 * GROUP, total - LANES), F32)
        stats = stats + turn(jnp.concatenate([piece, spare], axis=1), s * early)
        if late:
            piece = jnp.concatenate([got - piece, spare], axis=1)
            stats = stats + turn(piece, first_total - early + s * late)

    def weigh(top_row, end_row, lanes, target):
        size = end_row - top_row
        mine = stats[GROUP : GROUP + 1, :lanes] == merged[top_row:end_row]
        own_weights = []
        for h in range(GROUP):
            own = selfs[h][top_row:end_row]
            score = jnp.where(mine, stats[h : h + 1, :lanes], NEG)
            top = jnp.maximum(jnp.max(score, axis=1, keepdims=True), own)
            w = jnp.exp(score - top)
            own = jnp.exp(own - top)
            denominator = jnp.sum(w, axis=1, keepdims=True) + own
            w = w / denominator
            high = w.astype(BF16)
            target[h, :size] = high
            target[h, size:] = (w - high.astype(F32)).astype(BF16)
            own_weights.append(own / denominator)
        return own_weights

    def attend_to(h, merge, block, own_weights, top_row, end_row):
        size = end_row - top_row
        both = jnp.dot(merge[h], block, preferred_element_type=F32)
        result = both[:size] + both[size:] + latest_value[top_row:end_row] * own_weights[h]
        attended[top_row:end_row, h * HEAD_WIDTH : (h + 1) * HEAD_WIDTH] = result.astype(BF16)

    own_weights = weigh(0, early_rows, first_total, early_merge)
    for g in range(groups):
        for copy in slot_copies[g]:
            copy.wait()
        block = early_in[g].reshape(first_total, wide)
        for k in range(SUBGROUP):
            attend_to(
                g * SUBGROUP + k, early_merge, block[:, k * HEAD_WIDTH : (k + 1) * HEAD_WIDTH],
                own_weights, 0, early_rows,
            )
    loads[7].wait()

    def pass_on(k, slot, c, peer):
        return remote(
            z_out.at[k, c], z_in.at[slot, c], z_send.at[k, c], z_recv.at[slot, c], "kv", pos ^ peer
        )

    def project(top_row, end_row, offset):
        return jnp.dot(
            attended[top_row:end_row, :], weight[:, pl.ds(offset, half)],
            preferred_element_type=F32,
        )

    waves = []

    def project_rows(top_row, end_row):
        parts = range(top_row // CHUNK, end_row // CHUNK)
        waves.append(parts)

        def put(k, f, result):
            result = result.astype(BF16)
            for i, c in enumerate(parts):
                z_out[k, c, :, f * half : (f + 1) * half] = result[i * CHUNK : (i + 1) * CHUNK]

        for k in (3, 2, 1):
            for f in range(2):
                offset = pl.multiple_of((pos ^ k) * out_width + f * half, half)
                result = project(top_row, end_row, offset)
                if k == 1:
                    put(k, f, result)
                    continue

                @pl.when(inner == 0)
                def _():
                    put(k, f, result)

                @pl.when(inner == 1)
                def _():
                    terms[k - 2, top_row:end_row, f * half : (f + 1) * half] = result

            if k == 1:
                for c in parts:
                    pass_on(k, 0, c, 1).start()
            else:

                @pl.when(inner == 0)
                def _():
                    for c in parts:
                        pass_on(k, 5 - k, c, 1).start()

        for f in range(2):
            own_term[top_row:end_row, f * half : (f + 1) * half] = project(
                top_row, end_row, pl.multiple_of(pos * out_width + f * half, half)
            )

    project_rows(0, early_rows)
    if late:
        own_weights = weigh(early_rows, rows, total, late_merge)
        for g in range(groups):
            for copy in late_copies if g == 0 else []:
                copy.wait()
            for k in range(SUBGROUP):
                h = g * SUBGROUP + k
                cut = slice(h * HEAD_WIDTH, (h + 1) * HEAD_WIDTH)
                block = jnp.concatenate(
                    [
                        early_in[g, :, :, k * HEAD_WIDTH : (k + 1) * HEAD_WIDTH].reshape(
                            first_total, HEAD_WIDTH
                        ),
                        late_in[:, :, cut].reshape(n * late, HEAD_WIDTH),
                    ],
                    axis=0,
                )
                attend_to(h, late_merge, block, own_weights, early_rows, rows)
        project_rows(early_rows, rows)

    @pl.when(inner == 1)
    def _():
        for parts in waves:
            for k in (2, 3):
                for c in parts:
                    span = slice(c * CHUNK, (c + 1) * CHUNK)
                    pass_on(k, k, c, 1).wait_recv()
                    total_term = terms[k - 2, span, :] + z_in[k, c].astype(F32)
                    z_out[k, c] = total_term.astype(BF16)
                    pass_on(k, 1, c, k).start()

    for c in range(rows // CHUNK):
        span = slice(c * CHUNK, (c + 1) * CHUNK)
        pass_on(1, 0, c, 1).wait_recv()
        pass_on(1, 1, c, 1).wait_recv()
        result = own_term[span, :] + z_in[0, c].astype(F32) + z_in[1, c].astype(F32)
        final[span, :] = result.astype(BF16)
    for k in (1, 2, 3):
        for c in range(rows // CHUNK):
            pass_on(k, 0, c, 1).wait_send()

    out_ref[...] = jnp.dot(
        back[:, :rows], final[...], preferred_element_type=F32
    ).astype(BF16)
    for copy in sent:
        copy.wait_send()


def per_device(query, latest_key_value, cache, out_weight, home, pieces, lengths):
    n = lax.axis_size("req")
    kv = lax.axis_size("kv")
    rows, width = query.shape
    extra = pieces.shape[1] // n
    positions = cache.shape[1]
    pages = positions // PAGE_POSITIONS
    home_cap, guest_cap = 2 * rows // n, 2 * extra // n
    entries = -(-(home_cap + guest_cap) // 16) * 16
    early = 16 * (guest_cap // 16 + 1)
    early_homes = early - guest_cap
    early_rows = early_homes * (n // 2)
    if early >= entries or early_rows % CHUNK:
        early, early_homes, early_rows = entries, home_cap, rows
    late = max(entries - early, 16)
    plan = (n, entries, early, guest_cap, early_homes, early_rows)
    total = n * entries
    groups = GROUP // SUBGROUP
    out_width = out_weight.shape[1] // kv
    chunks = rows // CHUNK
    anywhere = pl.BlockSpec(memory_space=pl.ANY)
    dma = pltpu.SemaphoreType.DMA
    buffer = pltpu.VMEM
    return pl.pallas_call(
        functools.partial(kernel, n, kv, plan),
        name="paged_decode",
        out_shape=jax.ShapeDtypeStruct((rows, out_width), BF16),
        in_specs=[anywhere] * 7,
        out_specs=pl.BlockSpec(memory_space=pltpu.VMEM),
        scratch_shapes=[
            buffer(home.shape, I32),
            buffer(pieces.shape, I32),
            buffer(lengths.shape, I32),
            buffer(latest_key_value.shape, BF16),
            buffer((positions, HEAD_WIDTH), BF16),
            buffer((positions, HEAD_WIDTH), BF16),
            buffer(out_weight.shape, BF16),
            buffer((n, rows, width), BF16),
            buffer((pages * GROUP, HEAD_WIDTH), F32),
            buffer((pages * GROUP, HEAD_WIDTH), F32),
            buffer((pages * GROUP, LANES), F32),
            buffer((pages // LANES, GROUP, LANES), F32),
            buffer((pages // LANES, GROUP, LANES), F32),
            buffer((pages, n * rows), BF16),
            buffer((total, pages), BF16),
            buffer((rows, LANES), BF16),
            buffer((rows, LANES), BF16),
            buffer((groups, n, early, SUBGROUP * HEAD_WIDTH), BF16),
            buffer((groups, n, early, SUBGROUP * HEAD_WIDTH), BF16),
            buffer((n, late, width), BF16),
            buffer((n, late, width), BF16),
            buffer((n, 2 * GROUP, LANES), F32),
            buffer((n, 2 * GROUP, LANES), F32),
            buffer((GROUP, 2 * early_rows, n * early), BF16),
            buffer((GROUP, 2 * max(rows - early_rows, 16), total), BF16),
            buffer((rows, width), BF16),
            buffer((2, rows, out_width), F32),
            buffer((rows, out_width), F32),
            buffer((rows, out_width), BF16),
            buffer((4, chunks, CHUNK, out_width), BF16),
            buffer((4, chunks, CHUNK, out_width), BF16),
            dma((8,)),
            dma((max(13, n),)),
            dma((max(13, n),)),
            dma((groups + 2, n)),
            dma((groups + 2, n)),
            dma((4, chunks)),
            dma((4, chunks)),
        ],
        compiler_params=pltpu.CompilerParams(
            collective_id=1, has_side_effects=True, vmem_limit_bytes=60 << 20
        ),
    )(
        home,
        pieces,
        lengths,
        latest_key_value,
        query,
        cache,
        out_weight,
    )


def solution(mesh):
    placed = (
        P("req", "kv"),
        P(None, "req", "kv"),
        P(None, "req", "kv"),
        P("kv", None),
        P(),
        P(),
        P(),
    )
    return jax.shard_map(
        per_device, mesh=mesh, in_specs=placed, out_specs=P("req", "kv"), check_vma=False
    )
```

```python
import functools

import jax
import jax.numpy as jnp
from jax import lax
from jax.experimental import pallas as pl
from jax.experimental.pallas import tpu as pltpu
from jax.sharding import PartitionSpec as P

HEAD_WIDTH = 128
PAGE_POSITIONS = 128
MAX_SLOT_PAGES = 15
GROUP = 8
SUBGROUP = 2
LANES = 128
PAIRS = 64
CHUNK = 32
TURN_PAIRS = 16
SCALE = HEAD_WIDTH ** (-0.5)
NT = (((1,), (1,)), ((), ()))
NEG = float("-inf")
MESH = pl.DeviceIdType.MESH
F32, BF16, I32 = jnp.float32, jnp.bfloat16, jnp.int32


def iota(shape, dim):
    return lax.broadcasted_iota(I32, shape, dim)


def remote(src, dst, send_sem, recv_sem, axis, peer):
    return pltpu.make_async_remote_copy(
        src_ref=src,
        dst_ref=dst,
        send_sem=send_sem,
        recv_sem=recv_sem,
        device_id={axis: peer},
        device_id_type=MESH,
    )


def segment_scan(x, at, lane, width, combine, empty):
    ahead, behind = x, x
    shift = 1
    while shift < MAX_SLOT_PAGES:
        same = (pltpu.roll(at, shift, 1) == at) & (lane >= shift)
        ahead = combine(ahead, jnp.where(same, pltpu.roll(ahead, shift, 1), empty))
        same = (pltpu.roll(at, width - shift, 1) == at) & (lane < width - shift)
        behind = combine(behind, jnp.where(same, pltpu.roll(behind, width - shift, 1), empty))
        shift *= 2
    return ahead, behind


def pick(mask, row, axis):
    return jnp.sum(jnp.where(mask, row, 0.0), axis=axis, keepdims=True)


def page_tables(me, rows, extra, pages, plan, home, pieces, lengths):
    n, entries, early, guest_cap, early_homes, early_rows = plan
    batch, jobs = home.shape[1], pieces.shape[1]
    home_f, lengths = home.astype(F32), lengths.astype(F32)
    piece_req, piece_len = pieces[0:1].astype(F32), pieces[1:2].astype(F32)
    lane = iota((rows, batch), 1)
    mine = iota((rows, batch), 0) + me * rows
    my_home = pick(lane == mine, home_f, 1)
    hot = home == mine
    home_req = pick(hot, lane.astype(F32), 1)
    home_len = pick(hot, lengths, 1) - pick(piece_req == home_req, piece_len, 1)
    hot = iota((extra, jobs), 1) == iota((extra, jobs), 0) + me * extra
    guest_req, guest_len = pick(hot, piece_req, 1), pick(hot, piece_len, 1)
    count = -(-(rows + extra) // LANES) * LANES
    spare = count - rows - extra
    request = jnp.concatenate([home_req, guest_req, jnp.full((spare, 1), -1.0, F32)], axis=0)
    length = jnp.concatenate([home_len, guest_len, jnp.zeros((spare, 1), F32)], axis=0)
    my_home = jnp.concatenate([my_home, jnp.full((count - rows, 1), -1.0, F32)], axis=0)
    held_pages = jnp.floor((length + (PAGE_POSITIONS - 1)) * (1.0 / PAGE_POSITIONS))
    device = jnp.floor((request + 0.5) * (1.0 / rows))
    column = iota((count, LANES), 1)
    turned = jnp.where(column == 1, held_pages, jnp.where(column == 2, my_home, 0.0))
    turned = jnp.where(column == 0, device, turned).T
    slot, other = iota((count, count), 0), iota((count, count), 1)
    before = other < slot
    alike = jnp.where(slot < rows, 1, 0) == jnp.where(other < rows, 1, 0)
    rank = pick(before & alike & (turned[0:1] == device), 1.0, 1)
    begin = pick(before, turned[1:2], 1)
    rank = rank + jnp.where(iota((count, 1), 0) < rows, float(guest_cap), 0.0)
    late = n * early + device * (entries - early) + rank - early
    entry = jnp.where(rank < early, device * early + rank, late)
    page = iota((count, pages), 1).astype(F32)
    held = (begin <= page) & (page < begin + held_pages)
    left = jnp.clip(length - (page - begin) * PAGE_POSITIONS, 0.0, float(PAGE_POSITIONS))
    page_entry = pick(held, entry, 0)
    page_request = pick(held, request, 0)
    page_row = pick(held, request - device * rows + 1.0, 0)
    page_used = pick(held, left, 0)

    at_c, at_r = my_home[:LANES], turned[2:3, :LANES]
    owner_c = jnp.floor((at_c + 0.5) * (1.0 / rows))
    owner_r = jnp.floor((at_r + 0.5) * (1.0 / rows))
    sub, lane = iota((LANES, LANES), 0), iota((LANES, LANES), 1)
    same = owner_c == owner_r
    late_c = jnp.where(pick(same & (at_r < at_c), 1.0, 1) < early_homes, 0.0, 1.0)
    late_r = jnp.where(pick(same & (at_c < at_r), 1.0, 0) < early_homes, 0.0, 1.0)
    same = late_c == late_r
    turn_c = pick(same & (lane < sub), 1.0, 1) + late_c * early_rows
    turn_r = pick(same & (sub < lane), 1.0, 0) + late_r * early_rows
    there = (turn_r == sub.astype(F32)) & (lane < rows)
    there = jnp.where(there, 1.0, 0.0)[:rows]
    back = jnp.where(turn_c == lane.astype(F32), 1.0, 0.0)[:rows]
    merged = pick(there > 0.5, lane[:rows].astype(F32) + 1.0, 1)
    return page_entry, page_request, page_row, page_used, there, back, merged


def kernel(
    n, kv, plan,
    home_hbm, pieces_hbm, lengths_hbm, latest_hbm, query_hbm, cache_hbm, weight_hbm, out_ref,
    home, pieces, lengths, latest, keys, values, weight, q_all, q_buf, o_buf, used_buf,
    top_buf, sum_buf, hot_in, hot_out, there, back, early_out, early_in, late_out, late_in,
    stat_out, stat_in, early_merge, late_merge, attended, terms, own_term, final, z_out, z_in,
    load_sem, q_send, q_recv, s_send, s_recv, z_send, z_recv, *turned_keys,
):
    me, pos = lax.axis_index("req"), lax.axis_index("kv")
    _, entries, early, _, _, early_rows = plan
    rows, width = query_hbm.shape
    extra = pieces.shape[1] // n
    pages = cache_hbm.shape[1] // PAGE_POSITIONS
    total, first_total = n * entries, n * early
    late = entries - early
    groups = GROUP // SUBGROUP
    out_width = weight.shape[1] // kv
    half = out_width // 2

    barrier = pltpu.get_barrier_semaphore()
    for step in range(1, n):
        pl.semaphore_signal(barrier, inc=1, device_id={"req": me ^ step}, device_id_type=MESH)

    for step in (1, 2):
        pl.semaphore_signal(barrier, inc=1, device_id={"kv": pos ^ step}, device_id_type=MESH)
    inner = (pos + 1) // 2 % 2

    @pl.when(inner == 1)
    def _():
        pl.semaphore_signal(barrier, inc=1, device_id={"kv": pos ^ 3}, device_id_type=MESH)

    loads = [
        pltpu.make_async_copy(source, target, load_sem.at[i])
        for i, (source, target) in enumerate(
            [
                (query_hbm, q_all.at[0]),
                (home_hbm, home),
                (pieces_hbm, pieces),
                (lengths_hbm, lengths),
                (latest_hbm, latest),
                (cache_hbm.at[0], keys),
                (cache_hbm.at[1], values),
                (weight_hbm, weight),
            ]
        )
    ]
    for load in loads:
        load.start()
    loads[0].wait()
    pl.semaphore_wait(barrier, n + 1 + inner)

    def hand(block, part, parts, sem, peer):
        size = rows // parts
        span = slice(part * size, (part + 1) * size)
        return remote(
            q_all.at[block, span], q_all.at[block ^ peer, span],
            q_send.at[sem], q_recv.at[sem], "req", me ^ peer,
        )

    sent = []

    def begin(copy):
        copy.start()
        sent.append(copy)

    if n == 8:
        first = [hand(0, 0, 2, 1, 2), hand(0, 1, 2, 2, 4), hand(0, 1, 2, 3, 2), hand(0, 0, 2, 4, 4)]
    else:
        first = [hand(0, 0, 1, k, k) for k in range(2, n, 2)]
    for copy in first:
        begin(copy)
    sibling = hand(0, 0, 1, 0, 1)
    begin(sibling)

    for load in loads[1:5]:
        load.wait()
    page_entry, page_request, page_row, page_used, there_v, back_v, merged = page_tables(
        me, rows, extra, pages, plan,
        home[...].reshape(1, -1), pieces[...], lengths[...].reshape(1, -1),
    )
    there[...] = there_v.astype(BF16)
    back[...] = back_v.astype(BF16)
    line = iota((LANES, pages), 0)
    turned = jnp.where(line == 0, page_request, jnp.where(line == 1, page_used, 0.0)).T
    asked = turned[:, 0:1]
    owner = jnp.floor((asked + 0.5) * (1.0 / rows))
    place = asked.astype(I32) - owner.astype(I32) * rows + (owner.astype(I32) ^ me) * rows
    hot = place == iota((pages, n * rows), 1)
    hot_in[...] = jnp.where(hot, 1.0, 0.0).astype(BF16)
    used = jnp.broadcast_to(turned[:, 1:2], (pages, LANES))
    for h in range(GROUP):
        used_buf[pl.ds(h, pages, stride=GROUP), :] = used
    hot = page_entry.astype(I32) == iota((total, pages), 0)
    hot_out[...] = jnp.where(hot, 1.0, 0.0).astype(BF16)

    def gather(start, stop, more):
        block = q_all[start:stop].reshape((stop - start) * rows, width)
        hot = hot_in[:, start * rows : stop * rows]
        for h in range(GROUP):
            at = pl.ds(h, pages, stride=GROUP)
            q = jnp.dot(
                hot, block[:, h * HEAD_WIDTH : (h + 1) * HEAD_WIDTH], preferred_element_type=F32
            )
            q_buf[at, :] = q_buf[at, :] + q if more else q

    blocks = pages // (2 * TURN_PAIRS)
    stops = [blocks // 3, blocks * 5 // 6, blocks]

    def turn_keys(first_block, last_block):
        def body(i, carry):
            for j in range(TURN_PAIRS):
                at = pl.multiple_of((i * TURN_PAIRS + j) * 2 * PAGE_POSITIONS, 2 * PAGE_POSITIONS)
                both = keys[pl.ds(at, 2 * PAGE_POSITIONS), :].T
                turned_keys[0][pl.ds(at, HEAD_WIDTH), :] = both[:, :PAGE_POSITIONS]
                turned_keys[0][pl.ds(at + HEAD_WIDTH, HEAD_WIDTH), :] = both[:, PAGE_POSITIONS:]
            return carry

        if turned_keys:
            lax.fori_loop(first_block, last_block, body, 0)

    loads[5].wait()
    turn_keys(0, stops[0])
    if n == 8:
        first[0].wait_recv()
        begin(hand(2, 0, 2, 5, 4))
        begin(hand(2, 0, 2, 7, 1))
        first[1].wait_recv()
        begin(hand(4, 1, 2, 6, 2))
        begin(hand(4, 1, 2, 8, 1))
        turn_keys(stops[0], stops[1])
        first[2].wait_recv()
        begin(hand(2, 1, 2, 9, 1))
        first[3].wait_recv()
        begin(hand(4, 0, 2, 10, 1))
        turn_keys(stops[1], stops[2])
        sibling.wait_recv()
        for sem, block, part in ((7, 2, 0), (8, 4, 1), (9, 2, 1), (10, 4, 0)):
            hand(block, part, 2, sem, 1).wait_recv()
        gather(0, 6, False)
        hand(2, 0, 2, 5, 4).wait_recv()
        begin(hand(6, 0, 2, 11, 1))
        hand(4, 1, 2, 6, 2).wait_recv()
        begin(hand(6, 1, 2, 12, 1))
        for sem, part in ((11, 0), (12, 1)):
            hand(6, part, 2, sem, 1).wait_recv()
        gather(6, 8, True)
    else:
        for k in range(2, n, 2):
            first[k // 2 - 1].wait_recv()
            begin(hand(k, 0, 1, k + 1, 1))
        turn_keys(stops[0], stops[2])
        sibling.wait_recv()
        for k in range(2, n, 2):
            hand(k, 0, 1, k + 1, 1).wait_recv()
        gather(0, n, False)
    loads[6].wait()

    pair = 2 * GROUP
    span = 2 * PAGE_POSITIONS
    lane = iota((GROUP, LANES), 1)
    column = iota((pair, LANES), 1).astype(F32)
    upper = iota((pair, LANES), 0) < GROUP
    left_column = jnp.where(upper, column, 2.0 * span)
    right_column = jnp.where(upper, 2.0 * span, column)
    limit = jnp.concatenate([left_column, right_column], axis=1)
    ones = jnp.ones((span, LANES), BF16)

    def attend(chunk, carry):
        row0 = pl.multiple_of(chunk * (PAIRS * pair), PAIRS * pair)
        key0 = pl.multiple_of(chunk * (PAIRS * span), PAIRS * span)
        tops = jnp.zeros((GROUP, LANES), F32)
        sums = jnp.zeros((GROUP, LANES), F32)
        scores = []
        for j in range(PAIRS):
            q = q_buf[pl.ds(row0 + j * pair, pair), :].astype(BF16)
            if turned_keys:
                block = turned_keys[0][pl.ds(key0 + j * span, span), :]
                block = jnp.concatenate([block[:HEAD_WIDTH], block[HEAD_WIDTH:]], axis=1)
                scores.append(jnp.dot(q, block, preferred_element_type=F32))
            else:
                block = keys[pl.ds(key0 + j * span, span), :]
                scores.append(lax.dot_general(q, block, NT, preferred_element_type=F32))
        weights = []
        for j in range(PAIRS):
            filled = used_buf[pl.ds(row0 + j * pair, pair), :]
            in_use = limit < jnp.concatenate([filled, filled], axis=1)
            s = jnp.where(in_use, scores[j] * SCALE, NEG)
            top = jnp.max(s, axis=1, keepdims=True)
            weights.append(jnp.exp(s - top).astype(BF16))
            for k in range(2):
                tops = jnp.where(lane == 2 * j + k, top[k * GROUP : (k + 1) * GROUP], tops)
        totals = jnp.dot(jnp.concatenate(weights, axis=0), ones, preferred_element_type=F32)
        for p in range(2 * PAIRS):
            sums = jnp.where(lane == p, totals[p * GROUP : (p + 1) * GROUP], sums)
        for j in range(PAIRS):
            block = values[pl.ds(key0 + j * span, span), :]
            o_buf[pl.ds(row0 + j * pair, pair), :] = jnp.dot(
                weights[j], block, preferred_element_type=F32
            )
        top_buf[chunk] = tops
        sum_buf[chunk] = sums
        return carry

    lax.fori_loop(0, pages // (2 * PAIRS), attend, 0)

    chunks = pages // LANES
    top = jnp.concatenate([top_buf[c] for c in range(chunks)], axis=1)
    page_sum = jnp.concatenate([sum_buf[c] for c in range(chunks)], axis=1)
    at = jnp.broadcast_to(page_entry, (GROUP, pages))
    where = iota((GROUP, pages), 1)
    ahead, behind = segment_scan(top, at, where, pages, jnp.maximum, NEG)
    slot_top = jnp.maximum(ahead, behind)
    factor = jnp.exp(top - slot_top)
    part = page_sum * factor
    ahead, behind = segment_scan(part, at, where, pages, jnp.add, 0.0)
    slot_sum = jnp.maximum(ahead + behind - part, part)
    lse = slot_top + jnp.log(slot_sum)
    start = (where == 0) | (pltpu.roll(at, 1, 1) != at)
    start = jnp.where(start, 1.0, 0.0)
    high = lse.astype(BF16).astype(F32)
    rest = lse - high
    middle = rest.astype(BF16).astype(F32)
    low = rest - middle
    number = jnp.broadcast_to(page_row, (GROUP, pages))
    stacked = jnp.concatenate(
        [high * start, middle * start, low * start, number * start], axis=0
    ).astype(BF16)
    placed = lax.dot_general(stacked, hot_out[...], NT, preferred_element_type=F32)
    placed = jnp.concatenate(
        [
            placed[:GROUP] + placed[GROUP : 2 * GROUP] + placed[2 * GROUP : 3 * GROUP],
            placed[3 * GROUP :],
        ],
        axis=0,
    )
    column = iota((2 * GROUP, LANES), 1)

    def turn(x, by):
        by = by % total
        return pltpu.roll(x, by, 1) if by else x

    for b in range(n):
        piece = jnp.where(column < early, turn(placed, -b * early)[:, :LANES], 0.0)
        if late:
            other = turn(placed, early - first_total - b * late)[:, :LANES]
            piece = jnp.where((column >= early) & (column < entries), other, piece)
        stat_out[b] = piece

    def ship(source, target, index):
        copies = []
        for step in range(1, n):
            peer = lax.rem(me + step, n)
            copy = remote(
                source.at[peer], target.at[me],
                s_send.at[index, step], s_recv.at[index, step], "req", peer,
            )
            copy.start()
            copies.append(copy)
        target[me] = source[me]
        return copies

    stat_copies = ship(stat_out, stat_in, groups)
    ratio = jnp.concatenate(
        [factor / slot_sum, jnp.zeros((LANES - GROUP, pages), F32)], axis=0
    ).T
    slot_copies = []
    wide = SUBGROUP * HEAD_WIDTH
    for g in range(groups):
        block = jnp.concatenate(
            [
                (o_buf[pl.ds(h, pages, stride=GROUP), :] * ratio[:, h : h + 1]).astype(BF16)
                for h in range(g * SUBGROUP, (g + 1) * SUBGROUP)
            ],
            axis=1,
        )
        block = jnp.dot(hot_out[...], block, preferred_element_type=F32).astype(BF16)
        early_out[g] = block[:first_total].reshape(n, early, wide)
        slot_copies.append(ship(early_out.at[g], early_in.at[g], g))
        if late:
            late_out[:, :, g * wide : (g + 1) * wide] = block[first_total:].reshape(n, late, wide)
    if late:
        late_copies = ship(late_out, late_in, groups + 1)

    own_q = jnp.dot(there[:, :rows], q_all[0], preferred_element_type=F32)
    latest_key = jnp.dot(there[:, :rows], latest[0], preferred_element_type=F32)
    latest_value = jnp.dot(there[:, :rows], latest[1], preferred_element_type=F32)
    selfs = []
    for h in range(GROUP):
        q = own_q[:, h * HEAD_WIDTH : (h + 1) * HEAD_WIDTH]
        selfs.append(jnp.sum(q * latest_key, axis=1, keepdims=True) * SCALE)
    for copy in stat_copies:
        copy.wait()
    stats = jnp.zeros((2 * GROUP, total), F32)
    for s in range(n):
        got = stat_in[s]
        piece = jnp.where(column < early, got, 0.0)
        spare = jnp.zeros((2 * GROUP, total - LANES), F32)
        stats = stats + turn(jnp.concatenate([piece, spare], axis=1), s * early)
        if late:
            piece = jnp.concatenate([got - piece, spare], axis=1)
            stats = stats + turn(piece, first_total - early + s * late)

    def weigh(top_row, end_row, lanes, target):
        size = end_row - top_row
        mine = stats[GROUP : GROUP + 1, :lanes] == merged[top_row:end_row]
        own_weights = []
        for h in range(GROUP):
            own = selfs[h][top_row:end_row]
            score = jnp.where(mine, stats[h : h + 1, :lanes], NEG)
            top = jnp.maximum(jnp.max(score, axis=1, keepdims=True), own)
            w = jnp.exp(score - top)
            own = jnp.exp(own - top)
            denominator = jnp.sum(w, axis=1, keepdims=True) + own
            w = w / denominator
            high = w.astype(BF16)
            target[h, :size] = high
            target[h, size:] = (w - high.astype(F32)).astype(BF16)
            own_weights.append(own / denominator)
        return own_weights

    def attend_to(h, merge, block, own_weights, top_row, end_row):
        size = end_row - top_row
        both = jnp.dot(merge[h], block, preferred_element_type=F32)
        result = both[:size] + both[size:] + latest_value[top_row:end_row] * own_weights[h]
        attended[top_row:end_row, h * HEAD_WIDTH : (h + 1) * HEAD_WIDTH] = result.astype(BF16)

    own_weights = weigh(0, early_rows, first_total, early_merge)
    for g in range(groups):
        for copy in slot_copies[g]:
            copy.wait()
        block = early_in[g].reshape(first_total, wide)
        for k in range(SUBGROUP):
            attend_to(
                g * SUBGROUP + k, early_merge, block[:, k * HEAD_WIDTH : (k + 1) * HEAD_WIDTH],
                own_weights, 0, early_rows,
            )
    loads[7].wait()

    def pass_on(k, slot, c, peer):
        return remote(
            z_out.at[k, c], z_in.at[slot, c], z_send.at[k, c], z_recv.at[slot, c], "kv", pos ^ peer
        )

    def project(top_row, end_row, offset):
        return jnp.dot(
            attended[top_row:end_row, :], weight[:, pl.ds(offset, half)],
            preferred_element_type=F32,
        )

    waves = []

    def project_rows(top_row, end_row):
        parts = range(top_row // CHUNK, end_row // CHUNK)
        waves.append(parts)

        def put(k, f, result):
            result = result.astype(BF16)
            for i, c in enumerate(parts):
                z_out[k, c, :, f * half : (f + 1) * half] = result[i * CHUNK : (i + 1) * CHUNK]

        for k in (3, 2, 1):
            for f in range(2):
                offset = pl.multiple_of((pos ^ k) * out_width + f * half, half)
                result = project(top_row, end_row, offset)
                if k == 1:
                    put(k, f, result)
                    continue

                @pl.when(inner == 0)
                def _():
                    put(k, f, result)

                @pl.when(inner == 1)
                def _():
                    terms[k - 2, top_row:end_row, f * half : (f + 1) * half] = result

            if k == 1:
                for c in parts:
                    pass_on(k, 0, c, 1).start()
            else:

                @pl.when(inner == 0)
                def _():
                    for c in parts:
                        pass_on(k, 5 - k, c, 1).start()

        for f in range(2):
            own_term[top_row:end_row, f * half : (f + 1) * half] = project(
                top_row, end_row, pl.multiple_of(pos * out_width + f * half, half)
            )

    project_rows(0, early_rows)
    if late:
        own_weights = weigh(early_rows, rows, total, late_merge)
        for g in range(groups):
            for copy in late_copies if g == 0 else []:
                copy.wait()
            for k in range(SUBGROUP):
                h = g * SUBGROUP + k
                cut = slice(h * HEAD_WIDTH, (h + 1) * HEAD_WIDTH)
                block = jnp.concatenate(
                    [
                        early_in[g, :, :, k * HEAD_WIDTH : (k + 1) * HEAD_WIDTH].reshape(
                            first_total, HEAD_WIDTH
                        ),
                        late_in[:, :, cut].reshape(n * late, HEAD_WIDTH),
                    ],
                    axis=0,
                )
                attend_to(h, late_merge, block, own_weights, early_rows, rows)
        project_rows(early_rows, rows)

    @pl.when(inner == 1)
    def _():
        for parts in waves:
            for k in (2, 3):
                for c in parts:
                    span = slice(c * CHUNK, (c + 1) * CHUNK)
                    pass_on(k, k, c, 1).wait_recv()
                    total_term = terms[k - 2, span, :] + z_in[k, c].astype(F32)
                    z_out[k, c] = total_term.astype(BF16)
                    pass_on(k, 1, c, k).start()

    for c in range(rows // CHUNK):
        span = slice(c * CHUNK, (c + 1) * CHUNK)
        pass_on(1, 0, c, 1).wait_recv()
        pass_on(1, 1, c, 1).wait_recv()
        result = own_term[span, :] + z_in[0, c].astype(F32) + z_in[1, c].astype(F32)
        final[span, :] = result.astype(BF16)
    for k in (1, 2, 3):
        for c in range(rows // CHUNK):
            pass_on(k, 0, c, 1).wait_send()

    out_ref[...] = jnp.dot(
        back[:, :rows], final[...], preferred_element_type=F32
    ).astype(BF16)
    for copy in sent:
        copy.wait_send()


def per_device(query, latest_key_value, cache, out_weight, home, pieces, lengths):
    n = lax.axis_size("req")
    kv = lax.axis_size("kv")
    rows, width = query.shape
    extra = pieces.shape[1] // n
    positions = cache.shape[1]
    pages = positions // PAGE_POSITIONS
    home_cap, guest_cap = 2 * rows // n, 2 * extra // n
    entries = -(-(home_cap + guest_cap) // 16) * 16
    early = 16 * (guest_cap // 16 + 1)
    early_homes = early - guest_cap
    early_rows = early_homes * (n // 2)
    if early >= entries or early_rows % CHUNK:
        early, early_homes, early_rows = entries, home_cap, rows
    late = max(entries - early, 16)
    plan = (n, entries, early, guest_cap, early_homes, early_rows)
    total = n * entries
    groups = GROUP // SUBGROUP
    out_width = out_weight.shape[1] // kv
    chunks = rows // CHUNK
    anywhere = pl.BlockSpec(memory_space=pl.ANY)
    dma = pltpu.SemaphoreType.DMA
    buffer = pltpu.VMEM
    return pl.pallas_call(
        functools.partial(kernel, n, kv, plan),
        name="paged_decode",
        out_shape=jax.ShapeDtypeStruct((rows, out_width), BF16),
        in_specs=[anywhere] * 7,
        out_specs=pl.BlockSpec(memory_space=pltpu.VMEM),
        scratch_shapes=[
            buffer(home.shape, I32),
            buffer(pieces.shape, I32),
            buffer(lengths.shape, I32),
            buffer(latest_key_value.shape, BF16),
            buffer((positions, HEAD_WIDTH), BF16),
            buffer((positions, HEAD_WIDTH), BF16),
            buffer(out_weight.shape, BF16),
            buffer((n, rows, width), BF16),
            buffer((pages * GROUP, HEAD_WIDTH), F32),
            buffer((pages * GROUP, HEAD_WIDTH), F32),
            buffer((pages * GROUP, LANES), F32),
            buffer((pages // LANES, GROUP, LANES), F32),
            buffer((pages // LANES, GROUP, LANES), F32),
            buffer((pages, n * rows), BF16),
            buffer((total, pages), BF16),
            buffer((rows, LANES), BF16),
            buffer((rows, LANES), BF16),
            buffer((groups, n, early, SUBGROUP * HEAD_WIDTH), BF16),
            buffer((groups, n, early, SUBGROUP * HEAD_WIDTH), BF16),
            buffer((n, late, width), BF16),
            buffer((n, late, width), BF16),
            buffer((n, 2 * GROUP, LANES), F32),
            buffer((n, 2 * GROUP, LANES), F32),
            buffer((GROUP, 2 * early_rows, n * early), BF16),
            buffer((GROUP, 2 * max(rows - early_rows, 16), total), BF16),
            buffer((rows, width), BF16),
            buffer((2, rows, out_width), F32),
            buffer((rows, out_width), F32),
            buffer((rows, out_width), BF16),
            buffer((4, chunks, CHUNK, out_width), BF16),
            buffer((4, chunks, CHUNK, out_width), BF16),
            dma((8,)),
            dma((max(13, n),)),
            dma((max(13, n),)),
            dma((groups + 2, n)),
            dma((groups + 2, n)),
            dma((4, chunks)),
            dma((4, chunks)),
        ]
        + ([buffer((positions, HEAD_WIDTH), BF16)] if n <= 8 else []),
        compiler_params=pltpu.CompilerParams(
            collective_id=1, has_side_effects=True, vmem_limit_bytes=61 << 20
        ),
    )(
        home,
        pieces,
        lengths,
        latest_key_value,
        query,
        cache,
        out_weight,
    )


def solution(mesh):
    placed = (
        P("req", "kv"),
        P(None, "req", "kv"),
        P(None, "req", "kv"),
        P("kv", None),
        P(),
        P(),
        P(),
    )
    return jax.shard_map(
        per_device, mesh=mesh, in_specs=placed, out_specs=P("req", "kv"), check_vma=False
    )
```

```python
import functools

import jax
import jax.numpy as jnp
from jax import lax
from jax.experimental import pallas as pl
from jax.experimental.pallas import tpu as pltpu
from jax.sharding import PartitionSpec as P

HEAD_WIDTH = 128
PAGE_POSITIONS = 128
MAX_SLOT_PAGES = 15
GROUP = 8
SUBGROUP = 8
LANES = 128
PAIRS = 64
CHUNK = 32
TURN_PAIRS = 16
SCALE = HEAD_WIDTH ** (-0.5)
NT = (((1,), (1,)), ((), ()))
NEG = float("-inf")
MESH = pl.DeviceIdType.MESH
F32, BF16, I32 = jnp.float32, jnp.bfloat16, jnp.int32


def iota(shape, dim):
    return lax.broadcasted_iota(I32, shape, dim)


def remote(src, dst, send_sem, recv_sem, axis, peer):
    return pltpu.make_async_remote_copy(
        src_ref=src,
        dst_ref=dst,
        send_sem=send_sem,
        recv_sem=recv_sem,
        device_id={axis: peer},
        device_id_type=MESH,
    )


def segment_scan(x, at, lane, width, combine, empty):
    ahead, behind = x, x
    shift = 1
    while shift < MAX_SLOT_PAGES:
        same = (pltpu.roll(at, shift, 1) == at) & (lane >= shift)
        ahead = combine(ahead, jnp.where(same, pltpu.roll(ahead, shift, 1), empty))
        same = (pltpu.roll(at, width - shift, 1) == at) & (lane < width - shift)
        behind = combine(behind, jnp.where(same, pltpu.roll(behind, width - shift, 1), empty))
        shift *= 2
    return ahead, behind


def pick(mask, row, axis):
    return jnp.sum(jnp.where(mask, row, 0.0), axis=axis, keepdims=True)


def page_tables(me, rows, extra, pages, plan, home, pieces, lengths):
    n, entries, early, guest_cap, early_homes, early_rows = plan
    batch, jobs = home.shape[1], pieces.shape[1]
    home_f, lengths = home.astype(F32), lengths.astype(F32)
    piece_req, piece_len = pieces[0:1].astype(F32), pieces[1:2].astype(F32)
    lane = iota((rows, batch), 1)
    mine = iota((rows, batch), 0) + me * rows
    my_home = pick(lane == mine, home_f, 1)
    hot = home == mine
    home_req = pick(hot, lane.astype(F32), 1)
    home_len = pick(hot, lengths, 1) - pick(piece_req == home_req, piece_len, 1)
    hot = iota((extra, jobs), 1) == iota((extra, jobs), 0) + me * extra
    guest_req, guest_len = pick(hot, piece_req, 1), pick(hot, piece_len, 1)
    count = -(-(rows + extra) // LANES) * LANES
    spare = count - rows - extra
    request = jnp.concatenate([home_req, guest_req, jnp.full((spare, 1), -1.0, F32)], axis=0)
    length = jnp.concatenate([home_len, guest_len, jnp.zeros((spare, 1), F32)], axis=0)
    my_home = jnp.concatenate([my_home, jnp.full((count - rows, 1), -1.0, F32)], axis=0)
    held_pages = jnp.floor((length + (PAGE_POSITIONS - 1)) * (1.0 / PAGE_POSITIONS))
    device = jnp.floor((request + 0.5) * (1.0 / rows))
    column = iota((count, LANES), 1)
    turned = jnp.where(column == 1, held_pages, jnp.where(column == 2, my_home, 0.0))
    turned = jnp.where(column == 0, device, turned).T
    slot, other = iota((count, count), 0), iota((count, count), 1)
    before = other < slot
    alike = jnp.where(slot < rows, 1, 0) == jnp.where(other < rows, 1, 0)
    rank = pick(before & alike & (turned[0:1] == device), 1.0, 1)
    begin = pick(before, turned[1:2], 1)
    rank = rank + jnp.where(iota((count, 1), 0) < rows, float(guest_cap), 0.0)
    late = n * early + device * (entries - early) + rank - early
    entry = jnp.where(rank < early, device * early + rank, late)
    page = iota((count, pages), 1).astype(F32)
    held = (begin <= page) & (page < begin + held_pages)
    left = jnp.clip(length - (page - begin) * PAGE_POSITIONS, 0.0, float(PAGE_POSITIONS))
    page_entry = pick(held, entry, 0)
    page_request = pick(held, request, 0)
    page_row = pick(held, request - device * rows + 1.0, 0)
    page_used = pick(held, left, 0)

    at_c, at_r = my_home[:LANES], turned[2:3, :LANES]
    owner_c = jnp.floor((at_c + 0.5) * (1.0 / rows))
    owner_r = jnp.floor((at_r + 0.5) * (1.0 / rows))
    sub, lane = iota((LANES, LANES), 0), iota((LANES, LANES), 1)
    same = owner_c == owner_r
    late_c = jnp.where(pick(same & (at_r < at_c), 1.0, 1) < early_homes, 0.0, 1.0)
    late_r = jnp.where(pick(same & (at_c < at_r), 1.0, 0) < early_homes, 0.0, 1.0)
    same = late_c == late_r
    turn_c = pick(same & (lane < sub), 1.0, 1) + late_c * early_rows
    turn_r = pick(same & (sub < lane), 1.0, 0) + late_r * early_rows
    there = (turn_r == sub.astype(F32)) & (lane < rows)
    there = jnp.where(there, 1.0, 0.0)[:rows]
    back = jnp.where(turn_c == lane.astype(F32), 1.0, 0.0)[:rows]
    merged = pick(there > 0.5, lane[:rows].astype(F32) + 1.0, 1)
    return page_entry, page_request, page_row, page_used, there, back, merged


def kernel(
    n, kv, plan,
    home_hbm, pieces_hbm, lengths_hbm, latest_hbm, query_hbm, cache_hbm, weight_hbm, out_ref,
    home, pieces, lengths, latest, keys, values, weight, q_all, q_buf, o_buf, used_buf,
    top_buf, sum_buf, hot_in, hot_out, there, back, early_out, early_in, late_out, late_in,
    stat_out, stat_in, early_merge, late_merge, attended, terms, own_term, final, z_out, z_in,
    load_sem, q_send, q_recv, s_send, s_recv, z_send, z_recv, *turned_keys,
):
    me, pos = lax.axis_index("req"), lax.axis_index("kv")
    _, entries, early, _, _, early_rows = plan
    rows, width = query_hbm.shape
    extra = pieces.shape[1] // n
    pages = cache_hbm.shape[1] // PAGE_POSITIONS
    total, first_total = n * entries, n * early
    late = entries - early
    groups = GROUP // SUBGROUP
    out_width = weight.shape[1] // kv
    half = out_width // 2

    barrier = pltpu.get_barrier_semaphore()
    for step in range(1, n):
        pl.semaphore_signal(barrier, inc=1, device_id={"req": me ^ step}, device_id_type=MESH)

    for step in (1, 2):
        pl.semaphore_signal(barrier, inc=1, device_id={"kv": pos ^ step}, device_id_type=MESH)
    inner = (pos + 1) // 2 % 2

    @pl.when(inner == 1)
    def _():
        pl.semaphore_signal(barrier, inc=1, device_id={"kv": pos ^ 3}, device_id_type=MESH)

    loads = [
        pltpu.make_async_copy(source, target, load_sem.at[i])
        for i, (source, target) in enumerate(
            [
                (query_hbm, q_all.at[0]),
                (home_hbm, home),
                (pieces_hbm, pieces),
                (lengths_hbm, lengths),
                (latest_hbm, latest),
                (cache_hbm.at[0], keys),
                (cache_hbm.at[1], values),
                (weight_hbm, weight),
            ]
        )
    ]
    for load in loads:
        load.start()
    loads[0].wait()
    pl.semaphore_wait(barrier, n + 1 + inner)

    def hand(block, part, parts, sem, peer):
        size = rows // parts
        span = slice(part * size, (part + 1) * size)
        return remote(
            q_all.at[block, span], q_all.at[block ^ peer, span],
            q_send.at[sem], q_recv.at[sem], "req", me ^ peer,
        )

    sent = []

    def begin(copy):
        copy.start()
        sent.append(copy)

    if n == 8:
        first = [hand(0, 0, 2, 1, 2), hand(0, 1, 2, 2, 4), hand(0, 1, 2, 3, 2), hand(0, 0, 2, 4, 4)]
    else:
        first = [hand(0, 0, 1, k, k) for k in range(2, n, 2)]
    for copy in first:
        begin(copy)
    sibling = hand(0, 0, 1, 0, 1)
    begin(sibling)

    for load in loads[1:5]:
        load.wait()
    page_entry, page_request, page_row, page_used, there_v, back_v, merged = page_tables(
        me, rows, extra, pages, plan,
        home[...].reshape(1, -1), pieces[...], lengths[...].reshape(1, -1),
    )
    there[...] = there_v.astype(BF16)
    back[...] = back_v.astype(BF16)
    line = iota((LANES, pages), 0)
    turned = jnp.where(line == 0, page_request, jnp.where(line == 1, page_used, 0.0)).T
    asked = turned[:, 0:1]
    owner = jnp.floor((asked + 0.5) * (1.0 / rows))
    place = asked.astype(I32) - owner.astype(I32) * rows + (owner.astype(I32) ^ me) * rows
    hot = place == iota((pages, n * rows), 1)
    hot_in[...] = jnp.where(hot, 1.0, 0.0).astype(BF16)
    used = jnp.broadcast_to(turned[:, 1:2], (pages, LANES))
    for h in range(GROUP):
        used_buf[pl.ds(h, pages, stride=GROUP), :] = used
    hot = page_entry.astype(I32) == iota((total, pages), 0)
    hot_out[...] = jnp.where(hot, 1.0, 0.0).astype(BF16)

    def gather(start, stop, more):
        block = q_all[start:stop].reshape((stop - start) * rows, width)
        hot = hot_in[:, start * rows : stop * rows]
        for h in range(GROUP):
            at = pl.ds(h, pages, stride=GROUP)
            q = jnp.dot(
                hot, block[:, h * HEAD_WIDTH : (h + 1) * HEAD_WIDTH], preferred_element_type=F32
            )
            q_buf[at, :] = q_buf[at, :] + q if more else q

    blocks = pages // (2 * TURN_PAIRS)
    stops = [blocks // 3, blocks * 5 // 6, blocks]

    def turn_keys(first_block, last_block):
        def body(i, carry):
            for j in range(TURN_PAIRS):
                at = pl.multiple_of((i * TURN_PAIRS + j) * 2 * PAGE_POSITIONS, 2 * PAGE_POSITIONS)
                both = keys[pl.ds(at, 2 * PAGE_POSITIONS), :].T
                turned_keys[0][pl.ds(at, HEAD_WIDTH), :] = both[:, :PAGE_POSITIONS]
                turned_keys[0][pl.ds(at + HEAD_WIDTH, HEAD_WIDTH), :] = both[:, PAGE_POSITIONS:]
            return carry

        if turned_keys:
            lax.fori_loop(first_block, last_block, body, 0)

    loads[5].wait()
    turn_keys(0, stops[0])
    if n == 8:
        first[0].wait_recv()
        begin(hand(2, 0, 2, 5, 4))
        begin(hand(2, 0, 2, 7, 1))
        first[1].wait_recv()
        begin(hand(4, 1, 2, 6, 2))
        begin(hand(4, 1, 2, 8, 1))
        turn_keys(stops[0], stops[1])
        first[2].wait_recv()
        begin(hand(2, 1, 2, 9, 1))
        first[3].wait_recv()
        begin(hand(4, 0, 2, 10, 1))
        turn_keys(stops[1], stops[2])
        sibling.wait_recv()
        for sem, block, part in ((7, 2, 0), (8, 4, 1), (9, 2, 1), (10, 4, 0)):
            hand(block, part, 2, sem, 1).wait_recv()
        gather(0, 6, False)
        hand(2, 0, 2, 5, 4).wait_recv()
        begin(hand(6, 0, 2, 11, 1))
        hand(4, 1, 2, 6, 2).wait_recv()
        begin(hand(6, 1, 2, 12, 1))
        for sem, part in ((11, 0), (12, 1)):
            hand(6, part, 2, sem, 1).wait_recv()
        gather(6, 8, True)
    else:
        for k in range(2, n, 2):
            first[k // 2 - 1].wait_recv()
            begin(hand(k, 0, 1, k + 1, 1))
        turn_keys(stops[0], stops[2])
        sibling.wait_recv()
        for k in range(2, n, 2):
            hand(k, 0, 1, k + 1, 1).wait_recv()
        gather(0, n, False)
    loads[6].wait()

    pair = 2 * GROUP
    span = 2 * PAGE_POSITIONS
    lane = iota((GROUP, LANES), 1)
    column = iota((pair, LANES), 1).astype(F32)
    upper = iota((pair, LANES), 0) < GROUP
    left_column = jnp.where(upper, column, 2.0 * span)
    right_column = jnp.where(upper, 2.0 * span, column)
    limit = jnp.concatenate([left_column, right_column], axis=1)
    ones = jnp.ones((span, LANES), BF16)

    def attend(chunk, carry):
        row0 = pl.multiple_of(chunk * (PAIRS * pair), PAIRS * pair)
        key0 = pl.multiple_of(chunk * (PAIRS * span), PAIRS * span)
        tops = jnp.zeros((GROUP, LANES), F32)
        sums = jnp.zeros((GROUP, LANES), F32)
        scores = []
        for j in range(PAIRS):
            q = q_buf[pl.ds(row0 + j * pair, pair), :].astype(BF16)
            if turned_keys:
                block = turned_keys[0][pl.ds(key0 + j * span, span), :]
                block = jnp.concatenate([block[:HEAD_WIDTH], block[HEAD_WIDTH:]], axis=1)
                scores.append(jnp.dot(q, block, preferred_element_type=F32))
            else:
                block = keys[pl.ds(key0 + j * span, span), :]
                scores.append(lax.dot_general(q, block, NT, preferred_element_type=F32))
        weights = []
        for j in range(PAIRS):
            filled = used_buf[pl.ds(row0 + j * pair, pair), :]
            in_use = limit < jnp.concatenate([filled, filled], axis=1)
            s = jnp.where(in_use, scores[j] * SCALE, NEG)
            top = jnp.max(s, axis=1, keepdims=True)
            weights.append(jnp.exp(s - top).astype(BF16))
            for k in range(2):
                tops = jnp.where(lane == 2 * j + k, top[k * GROUP : (k + 1) * GROUP], tops)
        totals = jnp.dot(jnp.concatenate(weights, axis=0), ones, preferred_element_type=F32)
        for p in range(2 * PAIRS):
            sums = jnp.where(lane == p, totals[p * GROUP : (p + 1) * GROUP], sums)
        for j in range(PAIRS):
            block = values[pl.ds(key0 + j * span, span), :]
            o_buf[pl.ds(row0 + j * pair, pair), :] = jnp.dot(
                weights[j], block, preferred_element_type=F32
            )
        top_buf[chunk] = tops
        sum_buf[chunk] = sums
        return carry

    lax.fori_loop(0, pages // (2 * PAIRS), attend, 0)

    chunks = pages // LANES
    top = jnp.concatenate([top_buf[c] for c in range(chunks)], axis=1)
    page_sum = jnp.concatenate([sum_buf[c] for c in range(chunks)], axis=1)
    at = jnp.broadcast_to(page_entry, (GROUP, pages))
    where = iota((GROUP, pages), 1)
    ahead, behind = segment_scan(top, at, where, pages, jnp.maximum, NEG)
    slot_top = jnp.maximum(ahead, behind)
    factor = jnp.exp(top - slot_top)
    part = page_sum * factor
    ahead, behind = segment_scan(part, at, where, pages, jnp.add, 0.0)
    slot_sum = jnp.maximum(ahead + behind - part, part)
    lse = slot_top + jnp.log(slot_sum)
    start = (where == 0) | (pltpu.roll(at, 1, 1) != at)
    start = jnp.where(start, 1.0, 0.0)
    high = lse.astype(BF16).astype(F32)
    rest = lse - high
    middle = rest.astype(BF16).astype(F32)
    low = rest - middle
    number = jnp.broadcast_to(page_row, (GROUP, pages))
    stacked = jnp.concatenate(
        [high * start, middle * start, low * start, number * start], axis=0
    ).astype(BF16)
    placed = lax.dot_general(stacked, hot_out[...], NT, preferred_element_type=F32)
    placed = jnp.concatenate(
        [
            placed[:GROUP] + placed[GROUP : 2 * GROUP] + placed[2 * GROUP : 3 * GROUP],
            placed[3 * GROUP :],
        ],
        axis=0,
    )
    column = iota((2 * GROUP, LANES), 1)

    def turn(x, by):
        by = by % total
        return pltpu.roll(x, by, 1) if by else x

    for b in range(n):
        piece = jnp.where(column < early, turn(placed, -b * early)[:, :LANES], 0.0)
        if late:
            other = turn(placed, early - first_total - b * late)[:, :LANES]
            piece = jnp.where((column >= early) & (column < entries), other, piece)
        stat_out[b] = piece

    def ship(source, target, index):
        copies = []
        for step in range(1, n):
            peer = lax.rem(me + step, n)
            copy = remote(
                source.at[peer], target.at[me],
                s_send.at[index, step], s_recv.at[index, step], "req", peer,
            )
            copy.start()
            copies.append(copy)
        target[me] = source[me]
        return copies

    stat_copies = ship(stat_out, stat_in, groups)
    ratio = jnp.concatenate(
        [factor / slot_sum, jnp.zeros((LANES - GROUP, pages), F32)], axis=0
    ).T
    slot_copies = []
    wide = SUBGROUP * HEAD_WIDTH
    for g in range(groups):
        block = jnp.concatenate(
            [
                (o_buf[pl.ds(h, pages, stride=GROUP), :] * ratio[:, h : h + 1]).astype(BF16)
                for h in range(g * SUBGROUP, (g + 1) * SUBGROUP)
            ],
            axis=1,
        )
        block = jnp.dot(hot_out[...], block, preferred_element_type=F32).astype(BF16)
        early_out[g] = block[:first_total].reshape(n, early, wide)
        slot_copies.append(ship(early_out.at[g], early_in.at[g], g))
        if late:
            late_out[:, :, g * wide : (g + 1) * wide] = block[first_total:].reshape(n, late, wide)
    if late:
        late_copies = ship(late_out, late_in, groups + 1)

    own_q = jnp.dot(there[:, :rows], q_all[0], preferred_element_type=F32)
    latest_key = jnp.dot(there[:, :rows], latest[0], preferred_element_type=F32)
    latest_value = jnp.dot(there[:, :rows], latest[1], preferred_element_type=F32)
    selfs = []
    for h in range(GROUP):
        q = own_q[:, h * HEAD_WIDTH : (h + 1) * HEAD_WIDTH]
        selfs.append(jnp.sum(q * latest_key, axis=1, keepdims=True) * SCALE)
    for copy in stat_copies:
        copy.wait()
    stats = jnp.zeros((2 * GROUP, total), F32)
    for s in range(n):
        got = stat_in[s]
        piece = jnp.where(column < early, got, 0.0)
        spare = jnp.zeros((2 * GROUP, total - LANES), F32)
        stats = stats + turn(jnp.concatenate([piece, spare], axis=1), s * early)
        if late:
            piece = jnp.concatenate([got - piece, spare], axis=1)
            stats = stats + turn(piece, first_total - early + s * late)

    def weigh(top_row, end_row, lanes, target):
        size = end_row - top_row
        mine = stats[GROUP : GROUP + 1, :lanes] == merged[top_row:end_row]
        own_weights = []
        for h in range(GROUP):
            own = selfs[h][top_row:end_row]
            score = jnp.where(mine, stats[h : h + 1, :lanes], NEG)
            top = jnp.maximum(jnp.max(score, axis=1, keepdims=True), own)
            w = jnp.exp(score - top)
            own = jnp.exp(own - top)
            denominator = jnp.sum(w, axis=1, keepdims=True) + own
            w = w / denominator
            high = w.astype(BF16)
            target[h, :size] = high
            target[h, size:] = (w - high.astype(F32)).astype(BF16)
            own_weights.append(own / denominator)
        return own_weights

    def attend_to(h, merge, block, own_weights, top_row, end_row):
        size = end_row - top_row
        both = jnp.dot(merge[h], block, preferred_element_type=F32)
        result = both[:size] + both[size:] + latest_value[top_row:end_row] * own_weights[h]
        attended[top_row:end_row, h * HEAD_WIDTH : (h + 1) * HEAD_WIDTH] = result.astype(BF16)

    own_weights = weigh(0, early_rows, first_total, early_merge)
    for g in range(groups):
        for copy in slot_copies[g]:
            copy.wait()
        block = early_in[g].reshape(first_total, wide)
        for k in range(SUBGROUP):
            attend_to(
                g * SUBGROUP + k, early_merge, block[:, k * HEAD_WIDTH : (k + 1) * HEAD_WIDTH],
                own_weights, 0, early_rows,
            )
    loads[7].wait()

    def pass_on(k, slot, c, peer):
        return remote(
            z_out.at[k, c], z_in.at[slot, c], z_send.at[k, c], z_recv.at[slot, c], "kv", pos ^ peer
        )

    def project(top_row, end_row, offset):
        return jnp.dot(
            attended[top_row:end_row, :], weight[:, pl.ds(offset, half)],
            preferred_element_type=F32,
        )

    waves = []

    def project_rows(top_row, end_row):
        parts = range(top_row // CHUNK, end_row // CHUNK)
        waves.append(parts)

        def put(k, f, result):
            result = result.astype(BF16)
            for i, c in enumerate(parts):
                z_out[k, c, :, f * half : (f + 1) * half] = result[i * CHUNK : (i + 1) * CHUNK]

        for k in (3, 2, 1):
            for f in range(2):
                offset = pl.multiple_of((pos ^ k) * out_width + f * half, half)
                result = project(top_row, end_row, offset)
                if k == 1:
                    put(k, f, result)
                    continue

                @pl.when(inner == 0)
                def _():
                    put(k, f, result)

                @pl.when(inner == 1)
                def _():
                    terms[k - 2, top_row:end_row, f * half : (f + 1) * half] = result

            if k == 1:
                for c in parts:
                    pass_on(k, 0, c, 1).start()
            else:

                @pl.when(inner == 0)
                def _():
                    for c in parts:
                        pass_on(k, 5 - k, c, 1).start()

        for f in range(2):
            own_term[top_row:end_row, f * half : (f + 1) * half] = project(
                top_row, end_row, pl.multiple_of(pos * out_width + f * half, half)
            )

    project_rows(0, early_rows)
    if late:
        own_weights = weigh(early_rows, rows, total, late_merge)
        for g in range(groups):
            for copy in late_copies if g == 0 else []:
                copy.wait()
            for k in range(SUBGROUP):
                h = g * SUBGROUP + k
                cut = slice(h * HEAD_WIDTH, (h + 1) * HEAD_WIDTH)
                block = jnp.concatenate(
                    [
                        early_in[g, :, :, k * HEAD_WIDTH : (k + 1) * HEAD_WIDTH].reshape(
                            first_total, HEAD_WIDTH
                        ),
                        late_in[:, :, cut].reshape(n * late, HEAD_WIDTH),
                    ],
                    axis=0,
                )
                attend_to(h, late_merge, block, own_weights, early_rows, rows)
        project_rows(early_rows, rows)

    @pl.when(inner == 1)
    def _():
        for parts in waves:
            for k in (2, 3):
                for c in parts:
                    span = slice(c * CHUNK, (c + 1) * CHUNK)
                    pass_on(k, k, c, 1).wait_recv()
                    total_term = terms[k - 2, span, :] + z_in[k, c].astype(F32)
                    z_out[k, c] = total_term.astype(BF16)
                    pass_on(k, 1, c, k).start()

    for c in range(rows // CHUNK):
        span = slice(c * CHUNK, (c + 1) * CHUNK)
        pass_on(1, 0, c, 1).wait_recv()
        pass_on(1, 1, c, 1).wait_recv()
        result = own_term[span, :] + z_in[0, c].astype(F32) + z_in[1, c].astype(F32)
        final[span, :] = result.astype(BF16)
    for k in (1, 2, 3):
        for c in range(rows // CHUNK):
            pass_on(k, 0, c, 1).wait_send()

    out_ref[...] = jnp.dot(
        back[:, :rows], final[...], preferred_element_type=F32
    ).astype(BF16)
    for copy in sent:
        copy.wait_send()


def per_device(query, latest_key_value, cache, out_weight, home, pieces, lengths):
    n = lax.axis_size("req")
    kv = lax.axis_size("kv")
    rows, width = query.shape
    extra = pieces.shape[1] // n
    positions = cache.shape[1]
    pages = positions // PAGE_POSITIONS
    home_cap, guest_cap = 2 * rows // n, 2 * extra // n
    entries = -(-(home_cap + guest_cap) // 16) * 16
    early = 16 * (guest_cap // 16 + 1)
    early_homes = early - guest_cap
    early_rows = early_homes * (n // 2)
    if early >= entries or early_rows % CHUNK:
        early, early_homes, early_rows = entries, home_cap, rows
    late = max(entries - early, 16)
    plan = (n, entries, early, guest_cap, early_homes, early_rows)
    total = n * entries
    groups = GROUP // SUBGROUP
    out_width = out_weight.shape[1] // kv
    chunks = rows // CHUNK
    anywhere = pl.BlockSpec(memory_space=pl.ANY)
    dma = pltpu.SemaphoreType.DMA
    buffer = pltpu.VMEM
    return pl.pallas_call(
        functools.partial(kernel, n, kv, plan),
        name="paged_decode",
        out_shape=jax.ShapeDtypeStruct((rows, out_width), BF16),
        in_specs=[anywhere] * 7,
        out_specs=pl.BlockSpec(memory_space=pltpu.VMEM),
        scratch_shapes=[
            buffer(home.shape, I32),
            buffer(pieces.shape, I32),
            buffer(lengths.shape, I32),
            buffer(latest_key_value.shape, BF16),
            buffer((positions, HEAD_WIDTH), BF16),
            buffer((positions, HEAD_WIDTH), BF16),
            buffer(out_weight.shape, BF16),
            buffer((n, rows, width), BF16),
            buffer((pages * GROUP, HEAD_WIDTH), F32),
            buffer((pages * GROUP, HEAD_WIDTH), F32),
            buffer((pages * GROUP, LANES), F32),
            buffer((pages // LANES, GROUP, LANES), F32),
            buffer((pages // LANES, GROUP, LANES), F32),
            buffer((pages, n * rows), BF16),
            buffer((total, pages), BF16),
            buffer((rows, LANES), BF16),
            buffer((rows, LANES), BF16),
            buffer((groups, n, early, SUBGROUP * HEAD_WIDTH), BF16),
            buffer((groups, n, early, SUBGROUP * HEAD_WIDTH), BF16),
            buffer((n, late, width), BF16),
            buffer((n, late, width), BF16),
            buffer((n, 2 * GROUP, LANES), F32),
            buffer((n, 2 * GROUP, LANES), F32),
            buffer((GROUP, 2 * early_rows, n * early), BF16),
            buffer((GROUP, 2 * max(rows - early_rows, 16), total), BF16),
            buffer((rows, width), BF16),
            buffer((2, rows, out_width), F32),
            buffer((rows, out_width), F32),
            buffer((rows, out_width), BF16),
            buffer((4, chunks, CHUNK, out_width), BF16),
            buffer((4, chunks, CHUNK, out_width), BF16),
            dma((8,)),
            dma((max(13, n),)),
            dma((max(13, n),)),
            dma((groups + 2, n)),
            dma((groups + 2, n)),
            dma((4, chunks)),
            dma((4, chunks)),
        ]
        + ([buffer((positions, HEAD_WIDTH), BF16)] if n <= 8 else []),
        compiler_params=pltpu.CompilerParams(
            collective_id=1, has_side_effects=True, vmem_limit_bytes=61 << 20
        ),
    )(
        home,
        pieces,
        lengths,
        latest_key_value,
        query,
        cache,
        out_weight,
    )


def solution(mesh):
    placed = (
        P("req", "kv"),
        P(None, "req", "kv"),
        P(None, "req", "kv"),
        P("kv", None),
        P(),
        P(),
        P(),
    )
    return jax.shard_map(
        per_device, mesh=mesh, in_specs=placed, out_specs=P("req", "kv"), check_vma=False
    )
```
